128 devices in a mesh: rows: 32 (over y, z, core), rep: 4 (over x).
Axes of the slice: x: 4, y: 4, z: 4, core: 2. Of those that a mesh axis runs over, the one named last changes fastest.
Arguments:
- entity_table: float32 [65536, 400], P(('rows', 'rep')), may hold values from -3 to 3
- entity_state: float32 [65536], P(('rows', 'rep')), may hold values from 0.005 to 1
- relation_table: float32 [7424, 400], replicated, may hold values from -3 to 3
- relation_state: float32 [7424], replicated, may hold values from 0.05 to 2
- end_owner: int32 [131072, 2], P(('rows', 'rep')), may hold values from 0 to 127, all different within a row; in each aligned block of 1024 rows (0 to 1023, 1024 to 2047, ...) at most 40 rows name the same one
- end_row: int32 [131072, 2], P(('rows', 'rep')), may hold values from 0 to 511
- relation_id: int32 [131072], P(('rows', 'rep')), may hold values from 0 to 7423
- negative_owner: int32 [131072, 1], P(('rows', 'rep')), may hold values from 0 to 127; in each aligned block of 1024 rows (0 to 1023, 1024 to 2047, ...) at most 16 rows name the same one
- negative_row: int32 [131072], P(('rows', 'rep')), may hold values from 0 to 511
Outputs:
- new_entity_table: float32 [65536, 400], P(('rows', 'rep'))
- new_entity_state: float32 [65536], P(('rows', 'rep'))
- new_relation_table: float32 [7424, 400], replicated
- new_relation_state: float32 [7424], replicated
The draws below stay inside these ranges and needn't reach their ends.
Inputs may be any that keep to these rules, and one draw needn't show every extreme that they name: `end_owner`: in each edge the head's and the tail's owners differ. Among the edges of one device no owner is named more than 40 times, heads and tails counted together; in some device some owner is named exactly 40 times. `negative_owner`: among the negatives of one group no owner is named more than 16 times; in some group some owner is named exactly 16 times.
All inputs are finite; a program needn't handle non-finite values.
Results may differ from the reference program's by a relative error of at most 0.0003.
Values sent between devices are 32-bit elements; how exact they have to be, the bound alone decides.
No kernel may reach another device: no remote copies, remote signals or barrier semaphores. Data moves between devices by JAX's collectives and lax.ppermute only.
A program may use at most 256 MiB of HBM per device.

```python
import math
import jax
import jax.numpy as jnp
import numpy as np
from jax import lax

D = 400
REL = 7424
ENT_DEV = 512
EDGES_DEV = 1024
NEG = 1024
CAP = 40
NCAP = 16
ENTITIES = 65536
EDGES = 131072
NEGS = 131072
DEVICES = 128


def place_ends(array, stream_key, least, largest):
    place = [jax.random.randint(jax.random.fold_in(stream_key, axis), (), 0, length) for axis, length in enumerate(array.shape)]
    widest = array.shape.index(max(array.shape))
    neighbour = place[:widest] + [(place[widest] + 1) % array.shape[widest]] + place[widest + 1:]
    return array.at[tuple(place)].set(least).at[tuple(neighbour)].set(largest)


def block_levels(rng, extent, shards, least, largest):
    def one(axis_at, parts):
        draws = jax.random.uniform(jax.random.fold_in(jax.random.fold_in(rng, 6), axis_at), (parts,), jnp.float32, least / len(shards), largest / len(shards))
        return jnp.repeat(jnp.exp(draws), extent[axis_at] // parts).reshape((-1,) + (1,) * (len(extent) - axis_at - 1))

    level = one(*shards[0])
    for cut in shards[1:]:
        level = level * one(*cut)
    return level


def cumulative_ranks(number_of, slope):
    loads = [(1 << 20) // math.isqrt(standing ** slope) + 1 for standing in range(1, number_of + 1)]
    spread = 1 + sum(loads) // (1 << 30)
    return np.cumsum(np.array([max(1, weight // spread) for weight in loads]))


def skewed_ids(rng, extent, count, skew):
    listing = cumulative_ranks(count, skew)
    ticket = jax.random.randint(jax.random.fold_in(rng, 1), extent, 0, int(listing[count - 1]))
    rank = jnp.searchsorted(jnp.asarray(listing, jnp.int32), ticket, side="right")
    return jax.random.permutation(jax.random.fold_in(rng, 2), count)[rank].astype(jnp.int32)


def deal_out(stream_key, own, number, rows, count, top, limit, slope):
    ranking = jax.random.permutation(stream_key, count)
    crowded, ordinary = portions_of(count, rows * top, limit, slope, True), portions_of(count, rows * top, limit, slope, False)
    places = jnp.arange(count)

    def named(lengths, offset_by):
        used = int((lengths > 0).sum())
        fixed = max(1, used // 4)
        shifted = fixed + (places - fixed + offset_by * (used - fixed)) % max(1, count - fixed)
        return jnp.zeros((count,), jnp.int32).at[ranking[jnp.where(places < fixed, places, shifted)]].set(jnp.asarray(lengths, jnp.int32))

    lengths = jnp.where(number % 4 == 0, named(crowded, number // 4), named(ordinary, number - number // 4 - 1))
    mixed = jax.random.permutation(jax.random.fold_in(own, 3), count)
    source_of, taker = mixed[0:count // 2 * 2:2], mixed[1:count // 2 * 2:2]
    slack = jnp.minimum(lengths[source_of] - 1, limit - lengths[taker]) // 2
    slack = jnp.where((source_of == ranking[0]) | (taker == ranking[0]) | (lengths[taker] == 0), 0, jnp.maximum(slack, 0))
    shifted = jax.random.randint(jax.random.fold_in(own, 4), (count // 2,), 0, 1 << 20) % (slack + 1)
    lengths = lengths.at[source_of].add(-shifted).at[taker].add(shifted)
    labels = jnp.searchsorted(jnp.cumsum(lengths), jnp.arange(rows * top), side="right").astype(jnp.int32)
    listing = labels.reshape(top, rows).T
    listing = listing[jax.random.permutation(jax.random.fold_in(own, 1), rows)]
    offset_by = jax.random.randint(jax.random.fold_in(own, 2), (rows, 1), 0, top)
    return jnp.take_along_axis(listing, (jnp.arange(top)[None, :] + offset_by) % top, axis=1)


def portions_of(amount, total, most, lean, full):
    weights = [(1 << 20) // math.isqrt(rank ** lean) + 1 for rank in range(1, amount + 1)]
    largest = most if full else min(most, max(-(-total // amount), total * weights[0] // sum(weights)))
    least = 1 if total - largest >= amount - 1 else 0
    given, surplus = [largest] + [least] * (amount - 1), total - largest - least * (amount - 1)
    while surplus > 0:
        movable = [i for i in range(1, amount) if given[i] < largest] or [i for i in range(1, amount) if given[i] < most]
        whole, remaining = sum([weights[i] for i in movable]), surplus
        for i in movable:
            more = min(most - given[i], max(1, remaining * weights[i] // whole), surplus)
            given[i] = given[i] + more
            surplus = surplus - more
    return np.array(given)


def centred(stream_key, dims, scale, bound, split=(), kind=jnp.bfloat16):
    array = scale * jax.random.normal(stream_key, dims, jnp.float32)
    if split:
        array = array * block_levels(stream_key, dims, split, -0.22, 0.18)
    return jnp.clip(array, -bound, bound).astype(kind)


def setup_inputs(seed: int = 0) -> dict:
    key_list = jax.random.split(jax.random.key(seed), 10)
    entity_table = centred(key_list[0], (ENTITIES, D), 0.5, 3.0, ((0, 128),), jnp.float32)
    entity_state = jnp.clip(jnp.exp(math.log(1.0) - 5.2983174 * jax.random.uniform(key_list[1], (ENTITIES,), jnp.float32) ** block_levels(key_list[1], (ENTITIES,), ((0, 128),), -0.2, 0.2)), 0.005, 1.0)
    relation_table = centred(key_list[2], (REL, D), 0.5, 3.0, (), jnp.float32)
    relation_state = jnp.clip(jnp.exp(jax.random.uniform(key_list[3], (REL,), jnp.float32, math.log(0.05), math.log(2.0))), 0.05, 2.0)
    end_owner_keys = jax.random.split(jax.random.fold_in(key_list[4], 1), EDGES // EDGES_DEV)
    end_owner_turns = jax.random.permutation(jax.random.fold_in(key_list[4], 3), EDGES // EDGES_DEV)
    end_owner = jax.vmap(lambda own, number: deal_out(jax.random.fold_in(key_list[4], 2), own, number, EDGES_DEV, DEVICES, 2, CAP, 2))(end_owner_keys, end_owner_turns).reshape((EDGES, 2))
    end_row = place_ends(jax.random.randint(key_list[5], (EDGES, 2), 0, ENT_DEV), jax.random.fold_in(key_list[5], 1), 0, ENT_DEV - 1).astype(jnp.int32)
    relation_id = place_ends(skewed_ids(key_list[6], (EDGES,), REL, 1), jax.random.fold_in(key_list[6], 3), 0, REL - 1).astype(jnp.int32)
    negative_owner_keys = jax.random.split(jax.random.fold_in(key_list[7], 1), NEGS // NEG)
    negative_owner_turns = jax.random.permutation(jax.random.fold_in(key_list[7], 3), NEGS // NEG)
    negative_owner = jax.vmap(lambda own, number: deal_out(jax.random.fold_in(key_list[7], 2), own, number, NEG, DEVICES, 1, NCAP, 1))(negative_owner_keys, negative_owner_turns).reshape((NEGS, 1))
    negative_row = place_ends(jax.random.randint(key_list[8], (NEGS,), 0, ENT_DEV), jax.random.fold_in(key_list[8], 1), 0, ENT_DEV - 1).astype(jnp.int32)
    return dict(entity_table=entity_table, entity_state=entity_state, relation_table=relation_table, relation_state=relation_state, end_owner=end_owner, end_row=end_row, relation_id=relation_id, negative_owner=negative_owner, negative_row=negative_row)


learn_rate = 0.5
adagrad_eps = 1e-10

def adagrad(table, state, grad):
    new_state = state + lax.optimization_barrier(jnp.mean(grad * grad, axis=1))
    new_table = table - learn_rate * grad / (jnp.sqrt(new_state)[:, None] + adagrad_eps)
    return (new_table, new_state)

def reference(entity_table, entity_state, relation_table, relation_state, end_owner, end_row, relation_id, negative_owner, negative_row):
    head_id = (end_owner[:, 0] * ENT_DEV + end_row[:, 0]).astype(jnp.int32)
    tail_id = (end_owner[:, 1] * ENT_DEV + end_row[:, 1]).astype(jnp.int32)
    negative_id = (negative_owner[:, 0] * ENT_DEV + negative_row).astype(jnp.int32)
    high = lax.Precision.HIGHEST

    def group(carry, index):
        entity_grad, relation_grad = carry
        start = (index * EDGES_DEV).astype(jnp.int32)
        nstart = (index * NEG).astype(jnp.int32)
        heads = lax.dynamic_slice_in_dim(head_id, start, EDGES_DEV)
        tails = lax.dynamic_slice_in_dim(tail_id, start, EDGES_DEV)
        kinds = lax.dynamic_slice_in_dim(relation_id, start, EDGES_DEV)
        negs = lax.dynamic_slice_in_dim(negative_id, nstart, NEG)
        head_rows = entity_table[heads]
        tail_rows = entity_table[tails]
        rel_rows = relation_table[kinds]
        neg_rows = entity_table[negs]
        product = head_rows * rel_rows
        positive = lax.optimization_barrier(jnp.sum(product * tail_rows, axis=1))
        score = jnp.dot(product, neg_rows.T, precision=high, preferred_element_type=jnp.float32)
        dpos = -jax.nn.sigmoid(-positive)
        dneg = jax.nn.sigmoid(score) / NEG
        grad_product = dpos[:, None] * tail_rows + jnp.dot(dneg, neg_rows, precision=high, preferred_element_type=jnp.float32)
        grad_tail = dpos[:, None] * product
        grad_neg = jnp.dot(dneg.T, product, precision=high, preferred_element_type=jnp.float32)
        entity_grad = entity_grad.at[heads].add(grad_product * rel_rows)
        entity_grad = entity_grad.at[tails].add(grad_tail)
        entity_grad = entity_grad.at[negs].add(grad_neg)
        relation_grad = relation_grad.at[kinds].add(grad_product * head_rows)
        return ((entity_grad, relation_grad), None)
    start_carry = (jnp.zeros(entity_table.shape, jnp.float32), jnp.zeros(relation_table.shape, jnp.float32))
    (entity_grad, relation_grad), _ = lax.scan(group, start_carry, jnp.arange(DEVICES, dtype=jnp.int32))
    new_entity_table, new_entity_state = adagrad(entity_table, entity_state, entity_grad)
    new_relation_table, new_relation_state = adagrad(relation_table, relation_state, relation_grad)
    return (new_entity_table, new_entity_state, new_relation_table, new_relation_state)
```

```python
import functools
import jax
import jax.numpy as jnp
from jax import lax
from jax.experimental import pallas as pl
from jax.experimental.pallas import tpu as pltpu
from jax.sharding import PartitionSpec as P

learn_rate = 0.5
adagrad_eps = 1e-10

AXES = ("rows", "rep")
F32, BF16, I32 = jnp.float32, jnp.bfloat16, jnp.int32
NDEV = 128
ENT = 512
EDGE = 1024
NEG = 1024
CAP = 40
SLOTS = 56
OCT = SLOTS // 8
TILES = 3 * OCT + 1
REL = 7424
GROUPS = REL // 128
VMEM_LIMIT = 60 * 1024 * 1024


def dot(a, b, dims):
    return lax.dot_general(a, b, (dims, ((), ())), preferred_element_type=F32)


NN = ((1,), (0,))
NT = ((1,), (1,))
TN = ((0,), (0,))


def split(x):
    hi = x.astype(BF16)
    return hi, (x - hi.astype(F32)).astype(BF16)


def prep_kernel(owner_ref, row_ref, request_ref, addr_ref):
    upper = (
        lax.broadcasted_iota(I32, (128, 128), 0) < lax.broadcasted_iota(I32, (128, 128), 1)
    ).astype(BF16)
    device = lax.broadcasted_iota(I32, (NDEV, 128), 0)
    lane = lax.broadcasted_iota(I32, (128, 128), 0)

    def block(i, carry):
        count, low, high = carry
        count = jnp.where(i == 16, 0.0, count)
        first = jnp.where(i >= 16, CAP, 0)
        owner = owner_ref[pl.ds(i, 1), :]
        row = row_ref[pl.ds(i, 1), :]
        onehot = (device == owner).astype(F32)
        onehot_b = onehot.astype(BF16)
        earlier = dot(onehot_b, upper, NN) + count
        rank = jnp.sum(onehot * earlier, axis=0, keepdims=True).astype(I32) + first
        count = count + jnp.sum(onehot, axis=1, keepdims=True)
        at = lane == rank
        low = low + dot(onehot_b, jnp.where(at, (row & 255).astype(F32), 0.0).astype(BF16), NT)
        high = high + dot(onehot_b, jnp.where(at, (row >> 8).astype(F32), 0.0).astype(BF16), NT)
        addr_ref[pl.ds(i, 1), :] = owner * (32 * OCT) + (rank >> 3) * 32 + (rank & 7)
        return count, low, high

    zero = jnp.zeros((NDEV, 128), F32)
    _, low, high = lax.fori_loop(0, 24, block, (jnp.zeros((NDEV, 1), F32), zero, zero))
    request_ref[...] = (low + 256.0 * high).astype(I32)


def prep(owner, row):
    return pl.pallas_call(
        prep_kernel,
        out_shape=(
            jax.ShapeDtypeStruct((NDEV, 128), I32),
            jax.ShapeDtypeStruct((24, 128), I32),
        ),
        name="prep",
    )(owner, row)


def lookup_kernel(wanted_ref, table_ref, out_ref, hi_ref, lo_ref, onehot_ref):
    @pl.when(pl.program_id(0) == 0)
    def _():
        for t in range(4):
            width = 128 if t < 3 else 16
            part = table_ref[t * 128 : t * 128 + width, :]
            if t == 3:
                part = jnp.concatenate([part, jnp.zeros((112, ENT), F32)], axis=0)
            hi, lo = split(part.T)
            hi_ref[:, t * 128 : (t + 1) * 128] = hi
            lo_ref[:, t * 128 : (t + 1) * 128] = lo

    wanted = wanted_ref[...].reshape(16, 128)
    padded = jnp.concatenate([wanted, jnp.zeros((112, 128), I32)], axis=0)
    columns = padded.T
    lane = lax.broadcasted_iota(I32, (2 * SLOTS, ENT), 1)
    for p in range(8):
        column = jnp.concatenate(
            [columns[:SLOTS, 2 * p : 2 * p + 1], columns[:SLOTS, 2 * p + 1 : 2 * p + 2]], axis=0
        )
        onehot_ref[p * 2 * SLOTS : (p + 1) * 2 * SLOTS, :] = (
            (lane == column).astype(F32).astype(BF16)
        )
    onehot = onehot_ref[...]
    for t in range(4):
        lanes = slice(t * 128, (t + 1) * 128)
        rows = dot(onehot, hi_ref[:, lanes], NN) + dot(onehot, lo_ref[:, lanes], NN)
        rows = rows.reshape(16, OCT, 8, 128)
        if t < 3:
            for q in range(OCT):
                out_ref[:, q * 3 + t] = rows[:, q]
        else:
            rest = rows[:, 0]
            for q in range(1, OCT):
                rest = rest + pltpu.roll(rows[:, q], 16 * q, 2)
            out_ref[:, 3 * OCT] = rest


def lookup(wanted, table_t):
    return pl.pallas_call(
        lookup_kernel,
        grid=(8,),
        in_specs=[
            pl.BlockSpec((16, 1, 128), lambda i: (i, 0, 0)),
            pl.BlockSpec((400, ENT), lambda i: (0, 0)),
        ],
        out_specs=pl.BlockSpec((16, TILES, 8, 128), lambda i: (i, 0, 0, 0)),
        out_shape=jax.ShapeDtypeStruct((NDEV, TILES, 8, 128), F32),
        scratch_shapes=[
            pltpu.VMEM((ENT, 512), BF16),
            pltpu.VMEM((ENT, 512), BF16),
            pltpu.VMEM((16 * SLOTS, ENT), BF16),
        ],
        compiler_params=pltpu.CompilerParams(vmem_limit_bytes=VMEM_LIMIT),
        name="lookup",
    )(wanted, table_t)


BLOCK = 256


def math_kernel(
    addr_ref, pay_ref, rel_ref, grad_ref, rel_grad_ref,
    rows, rest, hr_hi, hr_lo, n_hi, n_lo, g_neg, sems,
):
    copies = [
        pltpu.make_async_copy(
            pay_ref.at[:, 3 * q : 3 * q + 3], rows.at[:, q, 0:3], sems.at[q]
        )
        for q in range(OCT)
    ]
    tail_copy = pltpu.make_async_copy(pay_ref.at[:, 3 * OCT], rest, sems.at[OCT])
    tail_copy.start()
    for copy in copies:
        copy.start()
    tail_copy.wait()
    lane = lax.broadcasted_iota(I32, (8, 8, 128), 2)

    def expand(i, _):
        part = rest[pl.ds(i * 8, 8)]
        for q in range(OCT):
            shifted = part if q == 0 else pltpu.roll(part, 128 - 16 * q, 2)
            rows[pl.ds(i * 8, 8), q, 3] = jnp.where(lane < 16, shifted, 0.0)
        return 0

    lax.fori_loop(0, 16, expand, 0)
    for copy in copies:
        copy.wait()
    flat = rows.reshape(NDEV * OCT * 32, 128)
    grad_flat = grad_ref.reshape(384 * 32, 128)

    def gather(i, _):
        for j in range(8):
            a = addr_ref[i >> 4, (i & 15) * 8 + j]
            grad_flat[pl.ds(i * 32 + j, 4, stride=8), :] = flat[pl.ds(a, 4, stride=8), :]
        return 0

    lax.fori_loop(0, 384, gather, 0, unroll=4)

    def prepare(b, _):
        octets = pl.ds(b * 32, 32)
        edges = pl.ds(b * BLOCK, BLOCK)
        for t in range(4):
            lanes = slice(t * 128, (t + 1) * 128)
            hr = grad_ref[octets, t].reshape(BLOCK, 128) * rel_ref[edges, lanes]
            hr_hi[edges, lanes], hr_lo[edges, lanes] = split(hr)
            neg = grad_ref[pl.ds(256 + b * 32, 32), t].reshape(BLOCK, 128)
            n_hi[edges, lanes], n_lo[edges, lanes] = split(neg)
        return 0

    lax.fori_loop(0, EDGE // BLOCK, prepare, 0)
    g_neg[...] = jnp.zeros_like(g_neg)

    def block(b, _):
        edges = pl.ds(b * BLOCK, BLOCK)
        octets = pl.ds(b * 32, 32)
        tails = pl.ds(128 + b * 32, 32)
        a_hi, a_lo = hr_hi[edges, :], hr_lo[edges, :]
        score = dot(a_hi, n_hi[...], NT) + dot(a_hi, n_lo[...], NT) + dot(a_lo, n_hi[...], NT)
        p_hi, p_lo = split(1.0 / (1.0 + jnp.exp(-score)))
        g_hr = dot(p_hi, n_hi[...], NN) + dot(p_hi, n_lo[...], NN) + dot(p_lo, n_hi[...], NN)
        g_neg[...] += dot(p_hi, a_hi, TN) + dot(p_hi, a_lo, TN) + dot(p_lo, a_hi, TN)
        total = jnp.zeros((BLOCK, 128), F32)
        for t in range(4):
            lanes = slice(t * 128, (t + 1) * 128)
            hr = grad_ref[octets, t].reshape(BLOCK, 128) * rel_ref[edges, lanes]
            total = total + hr * grad_ref[tails, t].reshape(BLOCK, 128)
        positive = jnp.sum(total, axis=1, keepdims=True)
        d_pos = -1.0 / (1.0 + jnp.exp(positive))
        for t in range(4):
            lanes = slice(t * 128, (t + 1) * 128)
            head = grad_ref[octets, t].reshape(BLOCK, 128)
            tail = grad_ref[tails, t].reshape(BLOCK, 128)
            rel = rel_ref[edges, lanes]
            g = d_pos * tail + g_hr[:, lanes] * (1.0 / NEG)
            rel_grad_ref[octets, t] = (g * head).reshape(32, 8, 128)
            grad_ref[tails, t] = (d_pos * (head * rel)).reshape(32, 8, 128)
            grad_ref[octets, t] = (g * rel).reshape(32, 8, 128)
        return 0

    lax.fori_loop(0, EDGE // BLOCK, block, 0)
    for t in range(4):
        lanes = slice(t * 128, (t + 1) * 128)
        grad_ref[256:384, t] = (g_neg[:, lanes] * (1.0 / NEG)).reshape(128, 8, 128)


def math(addr, arrived, rel_rows):
    return pl.pallas_call(
        math_kernel,
        in_specs=[
            pl.BlockSpec(memory_space=pltpu.SMEM),
            pl.BlockSpec(memory_space=pl.ANY),
            pl.BlockSpec(memory_space=pltpu.VMEM),
        ],
        out_specs=(
            pl.BlockSpec(memory_space=pltpu.VMEM),
            pl.BlockSpec(memory_space=pltpu.VMEM),
        ),
        out_shape=(
            jax.ShapeDtypeStruct((384, 4, 8, 128), F32),
            jax.ShapeDtypeStruct((128, 4, 8, 128), F32),
        ),
        scratch_shapes=[
            pltpu.VMEM((NDEV, OCT, 4, 8, 128), F32),
            pltpu.VMEM((NDEV, 8, 128), F32),
            pltpu.VMEM((EDGE, 512), BF16),
            pltpu.VMEM((EDGE, 512), BF16),
            pltpu.VMEM((NEG, 512), BF16),
            pltpu.VMEM((NEG, 512), BF16),
            pltpu.VMEM((NEG, 512), F32),
            pltpu.SemaphoreType.DMA((OCT + 1,)),
        ],
        compiler_params=pltpu.CompilerParams(vmem_limit_bytes=VMEM_LIMIT),
        name="math",
    )(addr, arrived, rel_rows)


def relation_kernel(id_ref, grad_ref, out_ref, rows, packed, sems):
    zero = jnp.zeros((16, 4, 8, 128), F32)

    def clear(g, _):
        rows[pl.ds(g * 16, 16)] = zero
        return 0

    lax.fori_loop(0, GROUPS, clear, 0)
    flat = rows.reshape(REL * 4, 128)
    grad_flat = grad_ref.reshape(128 * 32, 128)

    def add(i, _):
        for j in range(8):
            r = id_ref[i >> 4, (i & 15) * 8 + j]
            at = pl.ds((r >> 3) * 32 + (r & 7), 4, stride=8)
            flat[at, :] = flat[at, :] + grad_flat[pl.ds(i * 32 + j, 4, stride=8), :]
        return 0

    lax.fori_loop(0, 128, add, 0, unroll=2)

    def copy(g):
        return pltpu.make_async_copy(
            packed.at[g & 1], out_ref.at[g], sems.at[g & 1]
        )

    def pack(g, _):
        @pl.when(g >= 2)
        def _():
            copy(g - 2).wait()

        for t in range(3):
            packed[g & 1, pl.ds(t * 16, 16)] = rows[pl.ds(g * 16, 16), t]
        for half in range(2):
            rest = rows[g * 16 + half * 8, 3]
            for q in range(1, 8):
                rest = rest + pltpu.roll(rows[g * 16 + half * 8 + q, 3], 16 * q, 1)
            packed[g & 1, 48 + half] = rest
        copy(g).start()
        return 0

    lax.fori_loop(0, GROUPS, pack, 0)
    copy(GROUPS - 2).wait()
    copy(GROUPS - 1).wait()


def relation_sum(ids, grad):
    return pl.pallas_call(
        relation_kernel,
        in_specs=[
            pl.BlockSpec(memory_space=pltpu.SMEM),
            pl.BlockSpec(memory_space=pltpu.VMEM),
        ],
        out_specs=pl.BlockSpec(memory_space=pl.ANY),
        out_shape=jax.ShapeDtypeStruct((GROUPS, 50, 8, 128), F32),
        scratch_shapes=[
            pltpu.VMEM((REL // 8, 4, 8, 128), F32),
            pltpu.VMEM((2, 50, 8, 128), F32),
            pltpu.SemaphoreType.DMA((2,)),
        ],
        compiler_params=pltpu.CompilerParams(vmem_limit_bytes=VMEM_LIMIT),
        name="relation_sum",
    )(ids, grad)


def pack_kernel(addr_ref, grad_ref, out_ref, rows, rest, sems):
    zero = jnp.zeros((8, OCT, 4, 8, 128), F32)

    def clear(i, _):
        rows[pl.ds(i * 8, 8)] = zero
        return 0

    lax.fori_loop(0, 16, clear, 0)
    flat = rows.reshape(NDEV * OCT * 32, 128)
    grad_flat = grad_ref.reshape(384 * 32, 128)

    def scatter(i, _):
        for j in range(8):
            a = addr_ref[i >> 4, (i & 15) * 8 + j]
            flat[pl.ds(a, 4, stride=8), :] = grad_flat[pl.ds(i * 32 + j, 4, stride=8), :]
        return 0

    lax.fori_loop(0, 384, scatter, 0, unroll=4)
    copies = [
        pltpu.make_async_copy(
            rows.at[:, q, 0:3], out_ref.at[:, 3 * q : 3 * q + 3], sems.at[q]
        )
        for q in range(OCT)
    ]
    for copy in copies:
        copy.start()

    def pack(i, _):
        part = rows[pl.ds(i * 8, 8), 0, 3]
        for q in range(1, OCT):
            part = part + pltpu.roll(rows[pl.ds(i * 8, 8), q, 3], 16 * q, 2)
        rest[pl.ds(i * 8, 8)] = part
        return 0

    lax.fori_loop(0, 16, pack, 0)
    last = pltpu.make_async_copy(rest, out_ref.at[:, 3 * OCT], sems.at[OCT])
    last.start()
    for copy in copies:
        copy.wait()
    last.wait()


def pack_grads(addr, grads):
    return pl.pallas_call(
        pack_kernel,
        in_specs=[
            pl.BlockSpec(memory_space=pltpu.SMEM),
            pl.BlockSpec(memory_space=pltpu.VMEM),
        ],
        out_specs=pl.BlockSpec(memory_space=pl.ANY),
        out_shape=jax.ShapeDtypeStruct((NDEV, TILES, 8, 128), F32),
        scratch_shapes=[
            pltpu.VMEM((NDEV, OCT, 4, 8, 128), F32),
            pltpu.VMEM((NDEV, 8, 128), F32),
            pltpu.SemaphoreType.DMA((OCT + 1,)),
        ],
        compiler_params=pltpu.CompilerParams(vmem_limit_bytes=VMEM_LIMIT),
        name="pack_grads",
    )(addr, grads)


def entity_kernel(wanted_ref, pay_ref, table_ref, state_ref, new_table, new_state, hi, lo, total):
    step = pl.program_id(0)

    @pl.when(step == 0)
    def _():
        total[...] = jnp.zeros_like(total)

    for t in range(4):
        lanes = slice(t * 128, (t + 1) * 128)
        parts = []
        for q in range(OCT):
            if t < 3:
                parts.append(pay_ref[:, q * 3 + t])
            else:
                part = pay_ref[:, 3 * OCT]
                if q:
                    part = pltpu.roll(part, 128 - 16 * q, 2)
                lane = lax.broadcasted_iota(I32, (16, 8, 128), 2)
                parts.append(jnp.where(lane < 16, part, 0.0))
        x = jnp.stack(parts, axis=1).reshape(16 * SLOTS, 128)
        hi[:, lanes], lo[:, lanes] = split(x)
    row = lax.broadcasted_iota(I32, (ENT, 16 * SLOTS), 0)
    onehot = (row == wanted_ref[...].reshape(1, 16 * SLOTS)).astype(F32).astype(BF16)
    total[...] += dot(onehot, hi[...], NN) + dot(onehot, lo[...], NN)

    @pl.when(step == pl.num_programs(0) - 1)
    def _():
        grad = total[...].T[:400, :]
        state = state_ref[...] + jnp.sum(grad * grad, axis=0, keepdims=True) / 400.0
        new_state[...] = state
        new_table[...] = table_ref[...] - learn_rate * grad / (jnp.sqrt(state) + adagrad_eps)


def entity_update(wanted, arrived, table_t, state):
    return pl.pallas_call(
        entity_kernel,
        grid=(8,),
        in_specs=[
            pl.BlockSpec((1, 1, 16 * SLOTS), lambda i: (i, 0, 0)),
            pl.BlockSpec((16, TILES, 8, 128), lambda i: (i, 0, 0, 0)),
            pl.BlockSpec((400, ENT), lambda i: (0, 0)),
            pl.BlockSpec((1, ENT), lambda i: (0, 0)),
        ],
        out_specs=(
            pl.BlockSpec((400, ENT), lambda i: (0, 0)),
            pl.BlockSpec((1, ENT), lambda i: (0, 0)),
        ),
        out_shape=(
            jax.ShapeDtypeStruct((400, ENT), F32),
            jax.ShapeDtypeStruct((1, ENT), F32),
        ),
        scratch_shapes=[
            pltpu.VMEM((16 * SLOTS, 512), BF16),
            pltpu.VMEM((16 * SLOTS, 512), BF16),
            pltpu.VMEM((ENT, 512), F32),
        ],
        compiler_params=pltpu.CompilerParams(vmem_limit_bytes=VMEM_LIMIT),
        name="entity_update",
    )(wanted, arrived, table_t, state)


def relation_update_kernel(grad_ref, table_ref, state_ref, new_table, new_state):
    for g in range(2):
        lanes = slice(g * 128, (g + 1) * 128)
        parts = []
        for t in range(3):
            parts.append(grad_ref[g, t * 16 : (t + 1) * 16].reshape(128, 128).T)
        rest = []
        for half in range(2):
            part = grad_ref[g, 48 + half]
            for q in range(8):
                rest.append(part if q == 0 else pltpu.roll(part, 128 - 16 * q, 1))
        parts.append(jnp.concatenate(rest, axis=0).T[:16, :])
        grad = jnp.concatenate(parts, axis=0)
        state = state_ref[:, lanes] + jnp.sum(grad * grad, axis=0, keepdims=True) / 400.0
        new_state[:, lanes] = state
        new_table[:, lanes] = table_ref[:, lanes] - grad * (
            learn_rate / (jnp.sqrt(state) + adagrad_eps)
        )


def relation_update(grad, table_t, state):
    return pl.pallas_call(
        relation_update_kernel,
        grid=(GROUPS // 2,),
        in_specs=[
            pl.BlockSpec((2, 50, 8, 128), lambda i: (i, 0, 0, 0)),
            pl.BlockSpec((400, 256), lambda i: (0, i)),
            pl.BlockSpec((1, 256), lambda i: (0, i)),
        ],
        out_specs=(
            pl.BlockSpec((400, 256), lambda i: (0, i)),
            pl.BlockSpec((1, 256), lambda i: (0, i)),
        ),
        out_shape=(
            jax.ShapeDtypeStruct((400, REL), F32),
            jax.ShapeDtypeStruct((1, REL), F32),
        ),
        compiler_params=pltpu.CompilerParams(vmem_limit_bytes=VMEM_LIMIT),
        name="relation_update",
    )(grad, table_t, state)


def exchange(x):
    return lax.all_to_all(x, AXES, split_axis=0, concat_axis=0, tiled=True)


def per_device(
    entity_table,
    entity_state,
    relation_table,
    relation_state,
    end_owner,
    end_row,
    relation_id,
    negative_owner,
    negative_row,
):
    owner = jnp.concatenate([end_owner.T.reshape(16, 128), negative_owner.reshape(8, 128)])
    row = jnp.concatenate([end_row.T.reshape(16, 128), negative_row.reshape(8, 128)])
    request, addr = prep(owner, row)
    wanted = exchange(request.reshape(NDEV, 1, 128))
    looked = lookup(wanted, entity_table.T)
    arrived = exchange(looked)
    rel_rows = jnp.pad(relation_table[relation_id], ((0, 0), (0, 112)))
    grads, rel_grads = math(addr, arrived, rel_rows)
    relation_grad = relation_sum(relation_id.reshape(8, 128), rel_grads)
    total_grad = lax.psum(relation_grad, AXES)
    outgoing = pack_grads(addr, grads)
    incoming = exchange(outgoing)
    slots = wanted[:, 0, :SLOTS].reshape(8, 1, 16 * SLOTS)
    new_entity_table, new_entity_state = entity_update(
        slots, incoming, entity_table.T, entity_state.reshape(1, ENT)
    )
    new_relation_table, new_relation_state = relation_update(
        total_grad, relation_table.T, relation_state.reshape(1, REL)
    )
    return (
        new_entity_table.T,
        new_entity_state.reshape(ENT),
        new_relation_table.T,
        new_relation_state.reshape(REL),
    )


def solution(mesh):
    return jax.shard_map(
        per_device,
        mesh=mesh,
        in_specs=(
            P(AXES, None),
            P(AXES),
            P(),
            P(),
            P(AXES, None),
            P(AXES, None),
            P(AXES),
            P(AXES, None),
            P(AXES),
        ),
        out_specs=(P(AXES, None), P(AXES), P(), P()),
        check_vma=False,
    )
```

```python
import functools
import jax
import jax.numpy as jnp
from jax import lax
from jax.experimental import pallas as pl
from jax.experimental.pallas import tpu as pltpu
from jax.sharding import PartitionSpec as P

learn_rate = 0.5
adagrad_eps = 1e-10

AXES = ("rows", "rep")
F32, BF16, I32 = jnp.float32, jnp.bfloat16, jnp.int32
ENT = 512
WIDTH = 400
EDGE = 1024
NEG = 1024
GROUP = 32
MAIN = 22
OCT = 28
OVER = OCT - MAIN
MAIN_TILES = 3 * MAIN + 3
OVER_TILES = 3 * OVER + 1
REL = 7424
RELGROUPS = REL // 128
VMEM_LIMIT = 60 * 1024 * 1024
FLAG = 127


def dot(a, b, dims):
    return lax.dot_general(a, b, (dims, ((), ())), preferred_element_type=F32)


NN = ((1,), (0,))
NT = ((1,), (1,))
TN = ((0,), (0,))


def split(x):
    hi = x.astype(BF16)
    return hi, (x - hi.astype(F32)).astype(BF16)


def prep_kernel(end_owner, end_row, neg_owner, neg_row, request_ref, addr_ref):
    iota0 = lax.broadcasted_iota(I32, (128, 128), 0)
    upper = (iota0 < lax.broadcasted_iota(I32, (128, 128), 1)).astype(BF16)
    group = lax.broadcasted_iota(I32, (GROUP, 128), 0)
    double = lax.broadcasted_iota(I32, (2 * GROUP, 128), 0)
    count = jnp.zeros((GROUP, 1), F32)
    low = jnp.zeros((2 * GROUP, 128), F32)
    high = jnp.zeros((2 * GROUP, 128), F32)
    for i in range(24):
        lanes = slice((i & 7) * 128, (i & 7) * 128 + 128)
        if i < 16:
            owner = end_owner[i >> 3 : (i >> 3) + 1, lanes]
            row = end_row[i >> 3 : (i >> 3) + 1, lanes]
        else:
            owner = neg_owner[:, lanes]
            row = neg_row[i - 16 : i - 15, :]
        target = owner >> 2
        value = (owner & 3) * ENT + row
        onehot = (group == target).astype(F32)
        earlier = dot(onehot.astype(BF16), upper, NN) + count
        rank = jnp.sum(onehot * earlier, axis=0, keepdims=True).astype(I32)
        count = count + jnp.sum(onehot, axis=1, keepdims=True)
        wide = (double == 2 * target + (rank >> 7)).astype(F32).astype(BF16)
        at = iota0 == (rank & 127)
        low = low + dot(wide, jnp.where(at, (value & 255).astype(F32), 0.0).astype(BF16), NT)
        high = high + dot(wide, jnp.where(at, (value >> 8).astype(F32), 0.0).astype(BF16), NT)
        addr_ref[i : i + 1, :] = (target * OCT + (rank >> 3)) * 32 + (rank & 7)
    most = jnp.max(count, axis=0, keepdims=True)
    flag = (most > 8.0 * MAIN).astype(F32)
    lane = lax.broadcasted_iota(I32, (2 * GROUP, 128), 1)
    mark = (lane == FLAG) & ((double & 1) == 1)
    request_ref[...] = jnp.where(mark, flag, low + 256.0 * high).astype(I32)


def prep(end_owner, end_row, neg_owner, neg_row):
    return pl.pallas_call(
        prep_kernel,
        out_shape=(
            jax.ShapeDtypeStruct((2 * GROUP, 128), I32),
            jax.ShapeDtypeStruct((24, 128), I32),
        ),
        name="prep",
    )(end_owner, end_row, neg_owner, neg_row)


STEP = 4


def lookup_kernel(octets, first, wanted_ref, table_ref, out_ref, table, rows):
    step = pl.program_id(0)

    @pl.when(step == 0)
    def _():
        def turn(i, _):
            for t in range(4):
                width = 128 if t < 3 else 16
                for b in range(4):
                    part = table_ref[i, t * 128 : t * 128 + width, b * 128 : (b + 1) * 128]
                    if t == 3:
                        part = jnp.concatenate([part, jnp.zeros((112, 128), F32)], axis=0)
                    table[pl.ds(i * 64 + b * 16, 16), t] = part.T.reshape(16, 8, 128)
            return 0

        lax.fori_loop(0, 4, turn, 0)

    flat = table.reshape(256 * 32, 128)
    rows_flat = rows.reshape(STEP * octets * 32, 128)
    for d in range(STEP):
        g = step * STEP + d

        def fetch(q, _):
            k = (q + first) * 8
            for j in range(8):
                w = wanted_ref[2 * g + (k >> 7), (k & 127) + j]
                a = (w >> 3) * 32 + (w & 7)
                rows_flat[pl.ds((d * octets + q) * 32 + j, 4, stride=8), :] = flat[
                    pl.ds(a, 4, stride=8), :
                ]
            return 0

        lax.fori_loop(0, octets, fetch, 0, unroll=2)
    for q in range(octets):
        out_ref[:, 3 * q : 3 * q + 3] = rows[:, q, 0:3]
    for tile in range((octets + 7) // 8):
        rest = rows[:, tile * 8, 3]
        for q in range(tile * 8 + 1, min(octets, tile * 8 + 8)):
            rest = rest + pltpu.roll(rows[:, q, 3], 16 * (q & 7), 2)
        out_ref[:, 3 * octets + tile] = rest


def lookup(octets, first, wanted, tables):
    tiles = 3 * octets + (octets + 7) // 8
    return pl.pallas_call(
        functools.partial(lookup_kernel, octets, first),
        grid=(GROUP // STEP,),
        in_specs=[
            pl.BlockSpec(memory_space=pltpu.SMEM),
            pl.BlockSpec((4, WIDTH, ENT), lambda i: (0, 0, 0)),
        ],
        out_specs=pl.BlockSpec((STEP, tiles, 8, 128), lambda i: (i, 0, 0, 0)),
        out_shape=jax.ShapeDtypeStruct((GROUP, tiles, 8, 128), F32),
        scratch_shapes=[
            pltpu.VMEM((256, 4, 8, 128), F32),
            pltpu.VMEM((STEP, octets, 4, 8, 128), F32),
        ],
        compiler_params=pltpu.CompilerParams(vmem_limit_bytes=VMEM_LIMIT),
        name="lookup" if first == 0 else "lookup_over",
    )(wanted, tables)


BLOCK = 256


def math_kernel(
    addr_ref, flag_ref, pay_ref, over_ref, rel_ref, grad_ref, rel_grad_ref,
    rows, rest, hr_hi, hr_lo, n_hi, n_lo, g_neg, sems,
):
    def fill(source, octets, first, tile, sem):
        copies = [
            pltpu.make_async_copy(
                source.at[:, 3 * q : 3 * q + 3], rows.at[:, first + q, 0:3], sems.at[sem + 1 + q]
            )
            for q in range(octets)
        ]
        tiles = (octets + 7) // 8
        last = pltpu.make_async_copy(
            source.at[:, 3 * octets : 3 * octets + tiles],
            rest.at[:, tile : tile + tiles],
            sems.at[sem],
        )
        last.start()
        for copy in copies:
            copy.start()
        last.wait()
        lane = lax.broadcasted_iota(I32, (8, 8, 128), 2)

        def expand(i, _):
            for q in range(octets):
                part = rest[pl.ds(i * 8, 8), tile + (q >> 3)]
                if q & 7:
                    part = pltpu.roll(part, 128 - 16 * (q & 7), 2)
                rows[pl.ds(i * 8, 8), first + q, 3] = jnp.where(lane < 16, part, 0.0)
            return 0

        lax.fori_loop(0, GROUP // 8, expand, 0)
        for copy in copies:
            copy.wait()

    fill(pay_ref, MAIN, 0, 0, 0)

    @pl.when(flag_ref[0] > 0)
    def _():
        fill(over_ref, OVER, MAIN, 3, MAIN + 1)

    flat = rows.reshape(GROUP * OCT * 32, 128)
    grad_flat = grad_ref.reshape(384 * 32, 128)

    def gather(i, _):
        for j in range(8):
            a = addr_ref[i >> 4, (i & 15) * 8 + j]
            grad_flat[pl.ds(i * 32 + j, 4, stride=8), :] = flat[pl.ds(a, 4, stride=8), :]
        return 0

    lax.fori_loop(0, 384, gather, 0, unroll=4)

    def prepare(b, _):
        octets = pl.ds(b * 32, 32)
        edges = pl.ds(b * BLOCK, BLOCK)
        for t in range(4):
            lanes = slice(t * 128, (t + 1) * 128)
            hr = grad_ref[octets, t].reshape(BLOCK, 128) * rel_ref[edges, lanes]
            hr_hi[edges, lanes], hr_lo[edges, lanes] = split(hr)
            neg = grad_ref[pl.ds(256 + b * 32, 32), t].reshape(BLOCK, 128)
            n_hi[edges, lanes], n_lo[edges, lanes] = split(neg)
        return 0

    lax.fori_loop(0, EDGE // BLOCK, prepare, 0)
    g_neg[...] = jnp.zeros_like(g_neg)

    def block(b, _):
        edges = pl.ds(b * BLOCK, BLOCK)
        octets = pl.ds(b * 32, 32)
        tails = pl.ds(128 + b * 32, 32)
        a_hi, a_lo = hr_hi[edges, :], hr_lo[edges, :]
        score = dot(a_hi, n_hi[...], NT) + dot(a_hi, n_lo[...], NT) + dot(a_lo, n_hi[...], NT)
        p_hi, p_lo = split(1.0 / (1.0 + jnp.exp(-score)))
        g_hr = dot(p_hi, n_hi[...], NN) + dot(p_hi, n_lo[...], NN) + dot(p_lo, n_hi[...], NN)
        g_neg[...] += dot(p_hi, a_hi, TN) + dot(p_hi, a_lo, TN) + dot(p_lo, a_hi, TN)
        total = jnp.zeros((BLOCK, 128), F32)
        for t in range(4):
            lanes = slice(t * 128, (t + 1) * 128)
            hr = grad_ref[octets, t].reshape(BLOCK, 128) * rel_ref[edges, lanes]
            total = total + hr * grad_ref[tails, t].reshape(BLOCK, 128)
        positive = jnp.sum(total, axis=1, keepdims=True)
        d_pos = -1.0 / (1.0 + jnp.exp(positive))
        for t in range(4):
            lanes = slice(t * 128, (t + 1) * 128)
            head = grad_ref[octets, t].reshape(BLOCK, 128)
            tail = grad_ref[tails, t].reshape(BLOCK, 128)
            rel = rel_ref[edges, lanes]
            g = d_pos * tail + g_hr[:, lanes] * (1.0 / NEG)
            rel_grad_ref[octets, t] = (g * head).reshape(32, 8, 128)
            grad_ref[tails, t] = (d_pos * (head * rel)).reshape(32, 8, 128)
            grad_ref[octets, t] = (g * rel).reshape(32, 8, 128)
        return 0

    lax.fori_loop(0, EDGE // BLOCK, block, 0)
    for t in range(4):
        lanes = slice(t * 128, (t + 1) * 128)
        grad_ref[256:384, t] = (g_neg[:, lanes] * (1.0 / NEG)).reshape(128, 8, 128)


def math(addr, flag, arrived, over, rel_rows):
    return pl.pallas_call(
        math_kernel,
        in_specs=[
            pl.BlockSpec(memory_space=pltpu.SMEM),
            pl.BlockSpec(memory_space=pltpu.SMEM),
            pl.BlockSpec(memory_space=pl.ANY),
            pl.BlockSpec(memory_space=pl.ANY),
            pl.BlockSpec(memory_space=pltpu.VMEM),
        ],
        out_specs=(
            pl.BlockSpec(memory_space=pltpu.VMEM),
            pl.BlockSpec(memory_space=pltpu.VMEM),
        ),
        out_shape=(
            jax.ShapeDtypeStruct((384, 4, 8, 128), F32),
            jax.ShapeDtypeStruct((128, 4, 8, 128), F32),
        ),
        scratch_shapes=[
            pltpu.VMEM((GROUP, OCT, 4, 8, 128), F32),
            pltpu.VMEM((GROUP, 4, 8, 128), F32),
            pltpu.VMEM((EDGE, 512), BF16),
            pltpu.VMEM((EDGE, 512), BF16),
            pltpu.VMEM((NEG, 512), BF16),
            pltpu.VMEM((NEG, 512), BF16),
            pltpu.VMEM((NEG, 512), F32),
            pltpu.SemaphoreType.DMA((OCT + 2,)),
        ],
        compiler_params=pltpu.CompilerParams(vmem_limit_bytes=VMEM_LIMIT),
        name="math",
    )(addr, flag, arrived, over, rel_rows)


def relation_kernel(id_ref, grad_ref, out_ref, rows, packed, sems):
    zero = jnp.zeros((16, 4, 8, 128), F32)

    def clear(g, _):
        rows[pl.ds(g * 16, 16)] = zero
        return 0

    lax.fori_loop(0, RELGROUPS, clear, 0)
    flat = rows.reshape(REL * 4, 128)
    grad_flat = grad_ref.reshape(128 * 32, 128)

    def add(i, _):
        for j in range(8):
            r = id_ref[i >> 4, (i & 15) * 8 + j]
            at = pl.ds((r >> 3) * 32 + (r & 7), 4, stride=8)
            flat[at, :] = flat[at, :] + grad_flat[pl.ds(i * 32 + j, 4, stride=8), :]
        return 0

    lax.fori_loop(0, 128, add, 0, unroll=2)

    def copy(g):
        return pltpu.make_async_copy(
            packed.at[g & 1], out_ref.at[g], sems.at[g & 1]
        )

    def pack(g, _):
        @pl.when(g >= 2)
        def _():
            copy(g - 2).wait()

        for t in range(4):
            part = rows[pl.ds(g * 16, 16), t].reshape(128, 128).T
            if t < 3:
                packed[g & 1, pl.ds(t * 16, 16)] = part.reshape(16, 8, 128)
            else:
                packed[g & 1, 48:50] = part[:16].reshape(2, 8, 128)
        copy(g).start()
        return 0

    lax.fori_loop(0, RELGROUPS, pack, 0)
    copy(RELGROUPS - 2).wait()
    copy(RELGROUPS - 1).wait()


def relation_sum(ids, grad):
    return pl.pallas_call(
        relation_kernel,
        in_specs=[
            pl.BlockSpec(memory_space=pltpu.SMEM),
            pl.BlockSpec(memory_space=pltpu.VMEM),
        ],
        out_specs=pl.BlockSpec(memory_space=pl.ANY),
        out_shape=jax.ShapeDtypeStruct((RELGROUPS, 50, 8, 128), F32),
        scratch_shapes=[
            pltpu.VMEM((REL // 8, 4, 8, 128), F32),
            pltpu.VMEM((2, 50, 8, 128), F32),
            pltpu.SemaphoreType.DMA((2,)),
        ],
        compiler_params=pltpu.CompilerParams(vmem_limit_bytes=VMEM_LIMIT),
        name="relation_sum",
    )(ids, grad)


def pack_kernel(addr_ref, flag_ref, grad_ref, out_ref, over_ref, rows, rest, sems):
    zero = jnp.zeros((2, OCT, 4, 8, 128), F32)

    def clear(i, _):
        rows[pl.ds(i * 2, 2)] = zero
        return 0

    lax.fori_loop(0, GROUP // 2, clear, 0)
    flat = rows.reshape(GROUP * OCT * 32, 128)
    grad_flat = grad_ref.reshape(384 * 32, 128)

    def scatter(i, _):
        for j in range(8):
            a = addr_ref[i >> 4, (i & 15) * 8 + j]
            flat[pl.ds(a, 4, stride=8), :] = grad_flat[pl.ds(i * 32 + j, 4, stride=8), :]
        return 0

    lax.fori_loop(0, 384, scatter, 0, unroll=4)

    def send(target, octets, first, tile, sem):
        copies = [
            pltpu.make_async_copy(
                rows.at[:, first + q, 0:3], target.at[:, 3 * q : 3 * q + 3], sems.at[sem + 1 + q]
            )
            for q in range(octets)
        ]
        for copy in copies:
            copy.start()
        tiles = (octets + 7) // 8

        def pack(i, _):
            at = pl.ds(i * 8, 8)
            for n in range(tiles):
                part = rows[at, first + n * 8, 3]
                for q in range(n * 8 + 1, min(octets, n * 8 + 8)):
                    part = part + pltpu.roll(rows[at, first + q, 3], 16 * (q & 7), 2)
                rest[at, tile + n] = part
            return 0

        lax.fori_loop(0, GROUP // 8, pack, 0)
        last = pltpu.make_async_copy(
            rest.at[:, tile : tile + tiles],
            target.at[:, 3 * octets : 3 * octets + tiles],
            sems.at[sem],
        )
        last.start()
        for copy in copies:
            copy.wait()
        last.wait()

    send(out_ref, MAIN, 0, 0, 0)

    @pl.when(flag_ref[0] > 0)
    def _():
        send(over_ref, OVER, MAIN, 3, MAIN + 1)


def pack_grads(addr, flag, grads):
    return pl.pallas_call(
        pack_kernel,
        in_specs=[
            pl.BlockSpec(memory_space=pltpu.SMEM),
            pl.BlockSpec(memory_space=pltpu.SMEM),
            pl.BlockSpec(memory_space=pltpu.VMEM),
        ],
        out_specs=(
            pl.BlockSpec(memory_space=pl.ANY),
            pl.BlockSpec(memory_space=pl.ANY),
        ),
        out_shape=(
            jax.ShapeDtypeStruct((GROUP, MAIN_TILES, 8, 128), F32),
            jax.ShapeDtypeStruct((GROUP, OVER_TILES, 8, 128), F32),
        ),
        scratch_shapes=[
            pltpu.VMEM((GROUP, OCT, 4, 8, 128), F32),
            pltpu.VMEM((GROUP, 4, 8, 128), F32),
            pltpu.SemaphoreType.DMA((OCT + 2,)),
        ],
        compiler_params=pltpu.CompilerParams(vmem_limit_bytes=VMEM_LIMIT),
        name="pack_grads",
    )(addr, flag, grads)


SUM_STEP = 8


def row_sum_kernel(octets, wanted_ref, pay_ref, out_ref, hi, lo, total):
    step = pl.program_id(0)
    slots = SUM_STEP * octets * 8

    @pl.when(step == 0)
    def _():
        total[...] = jnp.zeros_like(total)

    lane = lax.broadcasted_iota(I32, (SUM_STEP, 8, 128), 2)
    for t in range(4):
        lanes = slice(t * 128, (t + 1) * 128)
        parts = []
        for q in range(octets):
            if t < 3:
                parts.append(pay_ref[:, q * 3 + t])
            else:
                part = pay_ref[:, 3 * octets + (q >> 3)]
                if q & 7:
                    part = pltpu.roll(part, 128 - 16 * (q & 7), 2)
                parts.append(jnp.where(lane < 16, part, 0.0))
        hi[:, lanes], lo[:, lanes] = split(jnp.stack(parts, axis=1).reshape(slots, 128))
    wanted = wanted_ref[...].reshape(1, slots)

    def add(i, _):
        row = lax.broadcasted_iota(I32, (ENT, slots), 0) + i * ENT
        onehot = (row == wanted).astype(F32).astype(BF16)
        total[i] = total[i] + (dot(onehot, hi[...], NN) + dot(onehot, lo[...], NN))
        return 0

    lax.fori_loop(0, 4, add, 0)

    @pl.when(step == pl.num_programs(0) - 1)
    def _():
        def turn(i, _):
            out_ref[i] = total[i].T[:WIDTH, :]
            return 0

        lax.fori_loop(0, 4, turn, 0)


def row_sum(octets, wanted, arrived):
    tiles = 3 * octets + (octets + 7) // 8
    slots = SUM_STEP * octets * 8
    return pl.pallas_call(
        functools.partial(row_sum_kernel, octets),
        grid=(GROUP // SUM_STEP,),
        in_specs=[
            pl.BlockSpec((1, 1, slots), lambda i: (i, 0, 0)),
            pl.BlockSpec((SUM_STEP, tiles, 8, 128), lambda i: (i, 0, 0, 0)),
        ],
        out_specs=pl.BlockSpec((4, WIDTH, ENT), lambda i: (0, 0, 0)),
        out_shape=jax.ShapeDtypeStruct((4, WIDTH, ENT), F32),
        scratch_shapes=[
            pltpu.VMEM((slots, 512), BF16),
            pltpu.VMEM((slots, 512), BF16),
            pltpu.VMEM((4, ENT, 512), F32),
        ],
        compiler_params=pltpu.CompilerParams(vmem_limit_bytes=VMEM_LIMIT),
        name="row_sum" if octets == MAIN else "row_sum_over",
    )(wanted, arrived)


def entity_kernel(grad_ref, table_ref, state_ref, new_table, new_state):
    grad = (grad_ref[0] + grad_ref[1]) + (grad_ref[2] + grad_ref[3])
    state = state_ref[...] + jnp.sum(grad * grad, axis=0, keepdims=True) / float(WIDTH)
    new_state[...] = state
    new_table[...] = table_ref[...] - learn_rate * grad / (jnp.sqrt(state) + adagrad_eps)


def entity_update(grads, table_t, state):
    return pl.pallas_call(
        entity_kernel,
        out_shape=(
            jax.ShapeDtypeStruct((WIDTH, ENT), F32),
            jax.ShapeDtypeStruct((1, ENT), F32),
        ),
        compiler_params=pltpu.CompilerParams(vmem_limit_bytes=VMEM_LIMIT),
        name="entity_update",
    )(grads, table_t, state)


def relation_update_kernel(grad_ref, table_ref, state_ref, new_table, new_state):
    step = pl.program_id(0)
    for g in range(2):
        lanes = slice(g * 128, (g + 1) * 128)
        at = pl.ds(step * 2 + g, 1)
        grad = grad_ref[g].reshape(WIDTH, 128)
        state = state_ref[at, :] + jnp.sum(grad * grad, axis=0, keepdims=True) / float(WIDTH)
        new_state[at, :] = state
        new_table[:, lanes] = table_ref[:, lanes] - grad * (
            learn_rate / (jnp.sqrt(state) + adagrad_eps)
        )


def relation_update(grad, table_t, state):
    return pl.pallas_call(
        relation_update_kernel,
        grid=(RELGROUPS // 2,),
        in_specs=[
            pl.BlockSpec((2, 50, 8, 128), lambda i: (i, 0, 0, 0)),
            pl.BlockSpec((WIDTH, 256), lambda i: (0, i)),
            pl.BlockSpec((RELGROUPS, 128), lambda i: (0, 0)),
        ],
        out_specs=(
            pl.BlockSpec((WIDTH, 256), lambda i: (0, i)),
            pl.BlockSpec((RELGROUPS, 128), lambda i: (0, 0)),
        ),
        out_shape=(
            jax.ShapeDtypeStruct((WIDTH, REL), F32),
            jax.ShapeDtypeStruct((RELGROUPS, 128), F32),
        ),
        compiler_params=pltpu.CompilerParams(vmem_limit_bytes=VMEM_LIMIT),
        name="relation_update",
    )(grad, table_t, state)


def exchange(x, axis):
    return lax.all_to_all(x, axis, split_axis=0, concat_axis=0, tiled=True)


def any_device(flag):
    largest = flag
    for k in (1, 2, 3):
        moved = lax.ppermute(flag, "rep", [(p, (p + k) % 4) for p in range(4)])
        largest = jnp.maximum(largest, moved)
    return largest


def per_device(
    entity_table,
    entity_state,
    relation_table,
    relation_state,
    end_owner,
    end_row,
    relation_id,
    negative_owner,
    negative_row,
):
    table_t = entity_table.T
    tables = lax.all_gather(table_t, "rep", axis=0, tiled=False)
    request, addr = prep(
        end_owner.T, end_row.T, negative_owner.reshape(1, NEG), negative_row.reshape(8, 128)
    )
    wanted = exchange(request.reshape(GROUP, 2, 128), "rows")
    flag = any_device(jnp.max(wanted[:, 1, FLAG]).reshape(1))
    over_now = flag[0] > 0
    wanted_rows = wanted.reshape(2 * GROUP, 128)
    arrived = exchange(lookup(MAIN, 0, wanted_rows, tables), "rows")
    over = lax.cond(
        over_now,
        lambda: exchange(lookup(OVER, MAIN, wanted_rows, tables), "rows"),
        lambda: jnp.zeros((GROUP, OVER_TILES, 8, 128), F32),
    )
    rel_rows = jnp.pad(relation_table[relation_id], ((0, 0), (0, 112)))
    grads, rel_grads = math(addr, flag, arrived, over, rel_rows)
    outgoing, outgoing_over = pack_grads(addr, flag, grads)
    incoming = exchange(outgoing, "rows")
    relation_grad = relation_sum(relation_id.reshape(8, 128), rel_grads)
    total_grad = lax.psum(relation_grad, AXES)
    slots = wanted.reshape(GROUP, 256)

    def ids(first, octets):
        part = slots[:, first * 8 : (first + octets) * 8]
        return part.reshape(GROUP // SUM_STEP, 1, SUM_STEP * octets * 8)

    summed = row_sum(MAIN, ids(0, MAIN), incoming)
    summed = lax.cond(
        over_now,
        lambda x: x + row_sum(OVER, ids(MAIN, OVER), exchange(outgoing_over, "rows")),
        lambda x: x,
        summed,
    )
    entity_grads = exchange(summed, "rep")
    new_entity_table, new_entity_state = entity_update(
        entity_grads, table_t, entity_state.reshape(1, ENT)
    )
    new_relation_table, new_relation_state = relation_update(
        total_grad, relation_table.T, relation_state.reshape(RELGROUPS, 128)
    )
    return (
        new_entity_table.T,
        new_entity_state.reshape(ENT),
        new_relation_table.T,
        new_relation_state.reshape(REL),
    )


def solution(mesh):
    return jax.shard_map(
        per_device,
        mesh=mesh,
        in_specs=(
            P(AXES, None),
            P(AXES),
            P(),
            P(),
            P(AXES, None),
            P(AXES, None),
            P(AXES),
            P(AXES, None),
            P(AXES),
        ),
        out_specs=(P(AXES, None), P(AXES), P(), P()),
        check_vma=False,
    )
```

```python
import functools
import jax
import jax.numpy as jnp
from jax import lax
from jax.experimental import pallas as pl
from jax.experimental.pallas import tpu as pltpu
from jax.sharding import PartitionSpec as P

learn_rate = 0.5
adagrad_eps = 1e-10

AXES = ("rows", "rep")
F32, BF16, I32 = jnp.float32, jnp.bfloat16, jnp.int32
ENT = 512
WIDTH = 400
EDGE = 1024
NEG = 1024
GROUP = 32
MAIN = 24
OCT = 28
OVER = OCT - MAIN
MAIN_TILES = 3 * MAIN + 3
OVER_TILES = 3 * OVER + 1
REL = 7424
RELGROUPS = REL // 128
SHARDS = 128
VMEM_LIMIT = 60 * 1024 * 1024
FLAG = 127
COUNT = 126


def dot(a, b, dims):
    return lax.dot_general(a, b, (dims, ((), ())), preferred_element_type=F32)


NN = ((1,), (0,))
NT = ((1,), (1,))
TN = ((0,), (0,))


def split(x):
    hi = x.astype(BF16)
    return hi, (x - hi.astype(F32)).astype(BF16)


def prep_kernel(me_ref, end_owner, end_row, neg_owner, neg_row, request_ref, addr_ref):
    iota0 = lax.broadcasted_iota(I32, (128, 128), 0)
    upper = (iota0 < lax.broadcasted_iota(I32, (128, 128), 1)).astype(BF16)
    group = lax.broadcasted_iota(I32, (GROUP, 128), 0)
    double = lax.broadcasted_iota(I32, (2 * GROUP, 128), 0)
    count = jnp.zeros((GROUP, 1), F32)
    low = jnp.zeros((2 * GROUP, 128), F32)
    high = jnp.zeros((2 * GROUP, 128), F32)
    for i in range(24):
        lanes = slice((i & 7) * 128, (i & 7) * 128 + 128)
        if i < 16:
            owner = end_owner[i >> 3 : (i >> 3) + 1, lanes]
            row = end_row[i >> 3 : (i >> 3) + 1, lanes]
        else:
            owner = neg_owner[:, lanes]
            row = neg_row[i - 16 : i - 15, :]
        target = owner >> 2
        near = (owner - me_ref[0]) & 3
        value = near * (4 * ENT) + (row >> 3) * 32 + (row & 7)
        onehot = (group == target).astype(F32)
        earlier = dot(onehot.astype(BF16), upper, NN) + count
        rank = jnp.sum(onehot * earlier, axis=0, keepdims=True).astype(I32)
        count = count + jnp.sum(onehot, axis=1, keepdims=True)
        wide = (double == 2 * target + (rank >> 7)).astype(F32).astype(BF16)
        at = iota0 == (rank & 127)
        low = low + dot(wide, jnp.where(at, (value & 255).astype(F32), 0.0).astype(BF16), NT)
        high = high + dot(wide, jnp.where(at, (value >> 8).astype(F32), 0.0).astype(BF16), NT)
        addr_ref[i : i + 1, :] = (target * OCT + (rank >> 3)) * 32 + (rank & 7)
    most = jnp.max(count, axis=0, keepdims=True)
    flag = (most > 8.0 * MAIN).astype(F32)
    lane = lax.broadcasted_iota(I32, (2 * GROUP, 128), 1)
    mark = (lane == FLAG) & ((double & 1) == 1)
    pair = lax.broadcasted_iota(I32, (2 * GROUP, GROUP), 0) >> 1
    same = pair == lax.broadcasted_iota(I32, (2 * GROUP, GROUP), 1)
    half = (2.0 * jnp.floor(count * 0.5), count)
    low_count = half[1] - half[0]
    counts = dot(same.astype(F32).astype(BF16), (half[0] * 0.5).astype(BF16), NN) * 2.0
    counts = counts + dot(same.astype(F32).astype(BF16), low_count.astype(BF16), NN)
    request = jnp.where(mark, flag, low + 256.0 * high)
    mark = (lane == COUNT) & ((double & 1) == 1)
    request_ref[...] = jnp.where(mark, counts, request).astype(I32)


def prep(me, end_owner, end_row, neg_owner, neg_row):
    return pl.pallas_call(
        prep_kernel,
        out_shape=(
            jax.ShapeDtypeStruct((2 * GROUP, 128), I32),
            jax.ShapeDtypeStruct((24, 128), I32),
        ),
        in_specs=[pl.BlockSpec(memory_space=pltpu.SMEM)]
        + [pl.BlockSpec(memory_space=pltpu.VMEM)] * 4,
        name="prep",
    )(me, end_owner, end_row, neg_owner, neg_row)


STEP = 4


def lookup_kernel(
    octets, first, wanted_ref, own, right, across_a, across_b, left, out_ref, table, rows
):
    step = pl.program_id(0)

    @pl.when(step == 0)
    def _():
        def turn(b, _):
            lanes = pl.ds(pl.multiple_of(b * 128, 128), 128)
            for i, parts in enumerate(((own,), (right,), (across_a, across_b), (left,))):
                height = WIDTH // len(parts)
                for t in range(4):
                    pieces, low, high = [], t * 128, min(t * 128 + 128, WIDTH)
                    for n, part in enumerate(parts):
                        start, stop = max(low, n * height), min(high, (n + 1) * height)
                        if start < stop:
                            pieces.append(part[start - n * height : stop - n * height, lanes])
                    if t == 3:
                        pieces.append(jnp.zeros((112, 128), F32))
                    block = pieces[0] if len(pieces) == 1 else jnp.concatenate(pieces, axis=0)
                    table[pl.ds(i * 64 + b * 16, 16), t] = block.T.reshape(16, 8, 128)
            return 0

        lax.fori_loop(0, 4, turn, 0)

    flat = table.reshape(256 * 32, 128)
    rows_flat = rows.reshape(STEP * octets * 32, 128)
    for d in range(STEP):
        g = step * STEP + d
        used = (wanted_ref[2 * g + 1, COUNT] + 7) >> 3
        used = jnp.clip(used - first, 0, octets)

        def fetch(q, _):
            k = (q + first) * 8
            line, lane = 2 * g + (k >> 7), k & 127
            for j in range(8):
                a = wanted_ref[line, lane + j]
                rows_flat[pl.ds((d * octets + q) * 32 + j, 4, stride=8), :] = flat[
                    pl.ds(a, 4, stride=8), :
                ]
            return 0

        lax.fori_loop(0, used, fetch, 0)

        def blank(q, _):
            rows[d, q, 3] = jnp.zeros((8, 128), F32)
            return 0

        lax.fori_loop(used, octets, blank, 0)
    for q in range(octets):
        out_ref[:, 3 * q : 3 * q + 3] = rows[:, q, 0:3]
    for tile in range((octets + 7) // 8):
        rest = rows[:, tile * 8, 3]
        for q in range(tile * 8 + 1, min(octets, tile * 8 + 8)):
            rest = rest + pltpu.roll(rows[:, q, 3], 16 * (q & 7), 2)
        out_ref[:, 3 * octets + tile] = rest


def lookup(octets, first, wanted, tables):
    tiles = 3 * octets + (octets + 7) // 8
    return pl.pallas_call(
        functools.partial(lookup_kernel, octets, first),
        grid=(GROUP // STEP,),
        in_specs=[pl.BlockSpec(memory_space=pltpu.SMEM)]
        + [pl.BlockSpec(x.shape, lambda i: (0, 0)) for x in tables],
        out_specs=pl.BlockSpec((STEP, tiles, 8, 128), lambda i: (i, 0, 0, 0)),
        out_shape=jax.ShapeDtypeStruct((GROUP, tiles, 8, 128), F32),
        scratch_shapes=[
            pltpu.VMEM((256, 4, 8, 128), F32),
            pltpu.VMEM((STEP, octets, 4, 8, 128), F32),
        ],
        compiler_params=pltpu.CompilerParams(vmem_limit_bytes=VMEM_LIMIT),
        name="lookup" if first == 0 else "lookup_over",
    )(wanted, *tables)


BLOCK = 256


def math_kernel(
    addr_ref, flag_ref, pay_ref, over_ref, rel_ref, grad_ref, rel_grad_ref,
    rows, rest, hr_hi, hr_lo, n_hi, n_lo, g_neg, sems,
):
    def fill(source, octets, first, tile, sem):
        copies = [
            pltpu.make_async_copy(
                source.at[:, 3 * q : 3 * q + 3], rows.at[:, first + q, 0:3], sems.at[sem + 1 + q]
            )
            for q in range(octets)
        ]
        tiles = (octets + 7) // 8
        last = pltpu.make_async_copy(
            source.at[:, 3 * octets : 3 * octets + tiles],
            rest.at[:, tile : tile + tiles],
            sems.at[sem],
        )
        last.start()
        for copy in copies:
            copy.start()
        last.wait()
        lane = lax.broadcasted_iota(I32, (8, 8, 128), 2)

        def expand(i, _):
            for q in range(octets):
                part = rest[pl.ds(i * 8, 8), tile + (q >> 3)]
                if q & 7:
                    part = pltpu.roll(part, 128 - 16 * (q & 7), 2)
                rows[pl.ds(i * 8, 8), first + q, 3] = jnp.where(lane < 16, part, 0.0)
            return 0

        lax.fori_loop(0, GROUP // 8, expand, 0)
        for copy in copies:
            copy.wait()

    fill(pay_ref, MAIN, 0, 0, 0)

    @pl.when(flag_ref[0] > 0)
    def _():
        fill(over_ref, OVER, MAIN, 3, MAIN + 1)

    flat = rows.reshape(GROUP * OCT * 32, 128)
    grad_flat = grad_ref.reshape(384 * 32, 128)

    def gather(i, _):
        for j in range(8):
            a = addr_ref[i >> 4, (i & 15) * 8 + j]
            grad_flat[pl.ds(i * 32 + j, 4, stride=8), :] = flat[pl.ds(a, 4, stride=8), :]
        return 0

    lax.fori_loop(0, 384, gather, 0, unroll=4)

    def prepare(b, _):
        octets = pl.ds(b * 32, 32)
        edges = pl.ds(b * BLOCK, BLOCK)
        for t in range(4):
            lanes = slice(t * 128, (t + 1) * 128)
            hr = grad_ref[octets, t].reshape(BLOCK, 128) * rel_ref[edges, lanes]
            hr_hi[edges, lanes], hr_lo[edges, lanes] = split(hr)
            neg = grad_ref[pl.ds(256 + b * 32, 32), t].reshape(BLOCK, 128)
            n_hi[edges, lanes], n_lo[edges, lanes] = split(neg)
        return 0

    lax.fori_loop(0, EDGE // BLOCK, prepare, 0)
    g_neg[...] = jnp.zeros_like(g_neg)

    def block(b, _):
        edges = pl.ds(b * BLOCK, BLOCK)
        octets = pl.ds(b * 32, 32)
        tails = pl.ds(128 + b * 32, 32)
        a_hi, a_lo = hr_hi[edges, :], hr_lo[edges, :]
        score = dot(a_hi, n_hi[...], NT) + dot(a_hi, n_lo[...], NT) + dot(a_lo, n_hi[...], NT)
        p_hi, p_lo = split(1.0 / (1.0 + jnp.exp(-score)))
        g_hr = dot(p_hi, n_hi[...], NN) + dot(p_hi, n_lo[...], NN) + dot(p_lo, n_hi[...], NN)
        g_neg[...] += dot(p_hi, a_hi, TN) + dot(p_hi, a_lo, TN) + dot(p_lo, a_hi, TN)
        total = jnp.zeros((BLOCK, 128), F32)
        for t in range(4):
            lanes = slice(t * 128, (t + 1) * 128)
            hr = grad_ref[octets, t].reshape(BLOCK, 128) * rel_ref[edges, lanes]
            total = total + hr * grad_ref[tails, t].reshape(BLOCK, 128)
        positive = jnp.sum(total, axis=1, keepdims=True)
        d_pos = -1.0 / (1.0 + jnp.exp(positive))
        for t in range(4):
            lanes = slice(t * 128, (t + 1) * 128)
            head = grad_ref[octets, t].reshape(BLOCK, 128)
            tail = grad_ref[tails, t].reshape(BLOCK, 128)
            rel = rel_ref[edges, lanes]
            g = d_pos * tail + g_hr[:, lanes] * (1.0 / NEG)
            rel_grad_ref[octets, t] = (g * head).reshape(32, 8, 128)
            grad_ref[tails, t] = (d_pos * (head * rel)).reshape(32, 8, 128)
            grad_ref[octets, t] = (g * rel).reshape(32, 8, 128)
        return 0

    lax.fori_loop(0, EDGE // BLOCK, block, 0)
    for t in range(4):
        lanes = slice(t * 128, (t + 1) * 128)
        grad_ref[256:384, t] = (g_neg[:, lanes] * (1.0 / NEG)).reshape(128, 8, 128)


def math(addr, flag, arrived, over, rel_rows):
    return pl.pallas_call(
        math_kernel,
        in_specs=[
            pl.BlockSpec(memory_space=pltpu.SMEM),
            pl.BlockSpec(memory_space=pltpu.SMEM),
            pl.BlockSpec(memory_space=pl.ANY),
            pl.BlockSpec(memory_space=pl.ANY),
            pl.BlockSpec(memory_space=pltpu.VMEM),
        ],
        out_specs=(
            pl.BlockSpec(memory_space=pltpu.VMEM),
            pl.BlockSpec(memory_space=pltpu.VMEM),
        ),
        out_shape=(
            jax.ShapeDtypeStruct((384, 4, 8, 128), F32),
            jax.ShapeDtypeStruct((128, 4, 8, 128), F32),
        ),
        scratch_shapes=[
            pltpu.VMEM((GROUP, OCT, 4, 8, 128), F32),
            pltpu.VMEM((GROUP, 4, 8, 128), F32),
            pltpu.VMEM((EDGE, 512), BF16),
            pltpu.VMEM((EDGE, 512), BF16),
            pltpu.VMEM((NEG, 512), BF16),
            pltpu.VMEM((NEG, 512), BF16),
            pltpu.VMEM((NEG, 512), F32),
            pltpu.SemaphoreType.DMA((OCT + 2,)),
        ],
        compiler_params=pltpu.CompilerParams(vmem_limit_bytes=VMEM_LIMIT),
        name="math",
    )(addr, flag, arrived, over, rel_rows)


def relation_kernel(id_ref, grad_ref, out_ref, rows, packed, sems):
    zero = jnp.zeros((16, 4, 8, 128), F32)

    def clear(g, _):
        rows[pl.ds(g * 16, 16)] = zero
        return 0

    lax.fori_loop(0, SHARDS // 2, clear, 0)
    flat = rows.reshape(SHARDS * 256, 128)
    grad_flat = grad_ref.reshape(128 * 32, 128)

    def add(i, _):
        for j in range(8):
            r = id_ref[i >> 4, (i & 15) * 8 + j]
            at = pl.ds((r >> 3) * 32 + (r & 7), 4, stride=8)
            flat[at, :] = flat[at, :] + grad_flat[pl.ds(i * 32 + j, 4, stride=8), :]
        return 0

    lax.fori_loop(0, 128, add, 0)

    def copy(g):
        return pltpu.make_async_copy(
            packed.at[g & 1], out_ref.at[pl.ds(g * 4, 4)], sems.at[g & 1]
        )

    def pack(g, _):
        @pl.when(g >= 2)
        def _():
            copy(g - 2).wait()

        for n in range(4):
            first = g * 32 + n * 8
            for t in range(3):
                packed[g & 1, n, t * 8 : t * 8 + 8] = rows[pl.ds(first, 8), t]
            rest = rows[first, 3]
            for q in range(1, 8):
                rest = rest + pltpu.roll(rows[first + q, 3], 16 * q, 1)
            packed[g & 1, n, 24] = rest
        copy(g).start()
        return 0

    lax.fori_loop(0, SHARDS // 4, pack, 0)
    copy(SHARDS // 4 - 2).wait()
    copy(SHARDS // 4 - 1).wait()


def relation_sum(ids, grad):
    return pl.pallas_call(
        relation_kernel,
        in_specs=[
            pl.BlockSpec(memory_space=pltpu.SMEM),
            pl.BlockSpec(memory_space=pltpu.VMEM),
        ],
        out_specs=pl.BlockSpec(memory_space=pl.ANY),
        out_shape=jax.ShapeDtypeStruct((SHARDS, 25, 8, 128), F32),
        scratch_shapes=[
            pltpu.VMEM((SHARDS * 8, 4, 8, 128), F32),
            pltpu.VMEM((2, 4, 25, 8, 128), F32),
            pltpu.SemaphoreType.DMA((2,)),
        ],
        compiler_params=pltpu.CompilerParams(vmem_limit_bytes=VMEM_LIMIT),
        name="relation_sum",
    )(ids, grad)


def pack_kernel(addr_ref, flag_ref, grad_ref, out_ref, over_ref, rows, rest, sems):
    zero = jnp.zeros((2, OCT, 4, 8, 128), F32)

    def clear(i, _):
        rows[pl.ds(i * 2, 2)] = zero
        return 0

    lax.fori_loop(0, GROUP // 2, clear, 0)
    flat = rows.reshape(GROUP * OCT * 32, 128)
    grad_flat = grad_ref.reshape(384 * 32, 128)

    def scatter(i, _):
        for j in range(8):
            a = addr_ref[i >> 4, (i & 15) * 8 + j]
            flat[pl.ds(a, 4, stride=8), :] = grad_flat[pl.ds(i * 32 + j, 4, stride=8), :]
        return 0

    lax.fori_loop(0, 384, scatter, 0, unroll=4)

    def send(target, octets, first, tile, sem):
        copies = [
            pltpu.make_async_copy(
                rows.at[:, first + q, 0:3], target.at[:, 3 * q : 3 * q + 3], sems.at[sem + 1 + q]
            )
            for q in range(octets)
        ]
        for copy in copies:
            copy.start()
        tiles = (octets + 7) // 8

        def pack(i, _):
            at = pl.ds(i * 8, 8)
            for n in range(tiles):
                part = rows[at, first + n * 8, 3]
                for q in range(n * 8 + 1, min(octets, n * 8 + 8)):
                    part = part + pltpu.roll(rows[at, first + q, 3], 16 * (q & 7), 2)
                rest[at, tile + n] = part
            return 0

        lax.fori_loop(0, GROUP // 8, pack, 0)
        last = pltpu.make_async_copy(
            rest.at[:, tile : tile + tiles],
            target.at[:, 3 * octets : 3 * octets + tiles],
            sems.at[sem],
        )
        last.start()
        for copy in copies:
            copy.wait()
        last.wait()

    send(out_ref, MAIN, 0, 0, 0)

    @pl.when(flag_ref[0] > 0)
    def _():
        send(over_ref, OVER, MAIN, 3, MAIN + 1)


def pack_grads(addr, flag, grads):
    return pl.pallas_call(
        pack_kernel,
        in_specs=[
            pl.BlockSpec(memory_space=pltpu.SMEM),
            pl.BlockSpec(memory_space=pltpu.SMEM),
            pl.BlockSpec(memory_space=pltpu.VMEM),
        ],
        out_specs=(
            pl.BlockSpec(memory_space=pl.ANY),
            pl.BlockSpec(memory_space=pl.ANY),
        ),
        out_shape=(
            jax.ShapeDtypeStruct((GROUP, MAIN_TILES, 8, 128), F32),
            jax.ShapeDtypeStruct((GROUP, OVER_TILES, 8, 128), F32),
        ),
        scratch_shapes=[
            pltpu.VMEM((GROUP, OCT, 4, 8, 128), F32),
            pltpu.VMEM((GROUP, 4, 8, 128), F32),
            pltpu.SemaphoreType.DMA((OCT + 2,)),
        ],
        compiler_params=pltpu.CompilerParams(vmem_limit_bytes=VMEM_LIMIT),
        name="pack_grads",
    )(addr, flag, grads)


SUM_STEP = 8


def row_sum_kernel(octets, wanted_ref, pay_ref, out_ref, hi, lo, total):
    step = pl.program_id(0)
    slots = SUM_STEP * octets * 8

    @pl.when(step == 0)
    def _():
        total[...] = jnp.zeros_like(total)

    lane = lax.broadcasted_iota(I32, (SUM_STEP, 8, 128), 2)
    for t in range(4):
        lanes = slice(t * 128, (t + 1) * 128)
        parts = []
        for q in range(octets):
            if t < 3:
                parts.append(pay_ref[:, q * 3 + t])
            else:
                part = pay_ref[:, 3 * octets + (q >> 3)]
                if q & 7:
                    part = pltpu.roll(part, 128 - 16 * (q & 7), 2)
                parts.append(jnp.where(lane < 16, part, 0.0))
        hi[:, lanes], lo[:, lanes] = split(jnp.stack(parts, axis=1).reshape(slots, 128))
    wanted = wanted_ref[...].reshape(1, slots)

    def add(i, _):
        row = lax.broadcasted_iota(I32, (ENT, slots), 0)
        row = i * (4 * ENT) + (row >> 3) * 32 + (row & 7)
        onehot = (row == wanted).astype(F32).astype(BF16)
        total[i] = total[i] + (dot(onehot, hi[...], NN) + dot(onehot, lo[...], NN))
        return 0

    lax.fori_loop(0, 4, add, 0)

    @pl.when(step == pl.num_programs(0) - 1)
    def _():
        def turn(i, _):
            out_ref[i] = total[i].T[:WIDTH, :]
            return 0

        lax.fori_loop(0, 4, turn, 0)


def row_sum(octets, wanted, arrived):
    tiles = 3 * octets + (octets + 7) // 8
    slots = SUM_STEP * octets * 8
    return pl.pallas_call(
        functools.partial(row_sum_kernel, octets),
        grid=(GROUP // SUM_STEP,),
        in_specs=[
            pl.BlockSpec((1, 1, slots), lambda i: (i, 0, 0)),
            pl.BlockSpec((SUM_STEP, tiles, 8, 128), lambda i: (i, 0, 0, 0)),
        ],
        out_specs=pl.BlockSpec((4, WIDTH, ENT), lambda i: (0, 0, 0)),
        out_shape=jax.ShapeDtypeStruct((4, WIDTH, ENT), F32),
        scratch_shapes=[
            pltpu.VMEM((slots, 512), BF16),
            pltpu.VMEM((slots, 512), BF16),
            pltpu.VMEM((4, ENT, 512), F32),
        ],
        compiler_params=pltpu.CompilerParams(vmem_limit_bytes=VMEM_LIMIT),
        name="row_sum" if octets == MAIN else "row_sum_over",
    )(wanted, arrived)


def entity_kernel(grad_ref, table_ref, state_ref, new_table, new_state):
    grad = (grad_ref[0] + grad_ref[1]) + (grad_ref[2] + grad_ref[3])
    state = state_ref[...] + jnp.sum(grad * grad, axis=0, keepdims=True) / float(WIDTH)
    new_state[...] = state
    new_table[...] = table_ref[...] - learn_rate * grad / (jnp.sqrt(state) + adagrad_eps)


def entity_update(grads, table_t, state):
    return pl.pallas_call(
        entity_kernel,
        out_shape=(
            jax.ShapeDtypeStruct((WIDTH, ENT), F32),
            jax.ShapeDtypeStruct((1, ENT), F32),
        ),
        compiler_params=pltpu.CompilerParams(vmem_limit_bytes=VMEM_LIMIT),
        name="entity_update",
    )(grads, table_t, state)


def relation_update_kernel(shard_ref, grad_ref, table_ref, state_ref, out_ref, table, sem):
    shard = shard_ref[0]
    group = jnp.minimum(shard >> 1, RELGROUPS - 1)
    lanes = pl.ds(pl.multiple_of(group * 128, 128), 128)
    copy = pltpu.make_async_copy(table_ref.at[:, lanes], table, sem)
    copy.start()
    odd = (shard & 1) == 1
    blank = jnp.zeros((64, 128), F32)
    parts = []
    for t in range(4):
        if t < 3:
            part = grad_ref[t * 8 : t * 8 + 8].reshape(64, 128)
        else:
            rest = grad_ref[24]
            part = jnp.concatenate(
                [rest] + [pltpu.roll(rest, 128 - 16 * q, 1) for q in range(1, 8)], axis=0
            )
        both = jnp.concatenate(
            [jnp.where(odd, 0.0, part), jnp.where(odd, part, 0.0)], axis=0
        ).T
        parts.append(both if t < 3 else both[:16])
    grad = jnp.concatenate(parts, axis=0)
    state = state_ref[pl.ds(group, 1), :]
    state = state + jnp.sum(grad * grad, axis=0, keepdims=True) / float(WIDTH)
    copy.wait()
    new = table[...] - grad * (learn_rate / (jnp.sqrt(state) + adagrad_eps))
    top, bottom = new[: WIDTH // 2], new[WIDTH // 2 :]
    low = lax.broadcasted_iota(I32, (WIDTH // 2, 128), 1) < 64
    even_rows = jnp.where(low, top, pltpu.roll(bottom, 64, 1))
    odd_rows = jnp.where(low, pltpu.roll(top, 64, 1), bottom)
    out_ref[0:25] = jnp.where(odd, odd_rows, even_rows).reshape(25, 8, 128)
    out_ref[25] = jnp.broadcast_to(state, (8, 128))


def relation_update(shard, grad, table_t, state):
    return pl.pallas_call(
        relation_update_kernel,
        in_specs=[
            pl.BlockSpec(memory_space=pltpu.SMEM),
            pl.BlockSpec(memory_space=pltpu.VMEM),
            pl.BlockSpec(memory_space=pl.ANY),
            pl.BlockSpec(memory_space=pltpu.VMEM),
        ],
        out_specs=pl.BlockSpec(memory_space=pltpu.VMEM),
        out_shape=jax.ShapeDtypeStruct((26, 8, 128), F32),
        scratch_shapes=[pltpu.VMEM((WIDTH, 128), F32), pltpu.SemaphoreType.DMA],
        compiler_params=pltpu.CompilerParams(vmem_limit_bytes=VMEM_LIMIT),
        name="relation_update",
    )(shard, grad, table_t, state)


def unpack_kernel(shards_ref, new_table, new_state):
    low = lax.broadcasted_iota(I32, (WIDTH // 2, 128), 1) < 64
    for g in range(2):
        lanes = slice(g * 128, (g + 1) * 128)
        even = shards_ref[2 * g, 0, 0:25].reshape(WIDTH // 2, 128)
        odd = shards_ref[2 * g + 1, 0, 0:25].reshape(WIDTH // 2, 128)
        new_table[: WIDTH // 2, lanes] = jnp.where(low, even, pltpu.roll(odd, 64, 1))
        new_table[WIDTH // 2 :, lanes] = jnp.where(low, pltpu.roll(even, 64, 1), odd)
        state = jnp.where(low[:8], shards_ref[2 * g, 0, 25], shards_ref[2 * g + 1, 0, 25])
        new_state[pl.ds(pl.program_id(0) * 2 + g, 1), :] = state[0:1]


def unpack(shards):
    return pl.pallas_call(
        unpack_kernel,
        grid=(RELGROUPS // 2,),
        in_specs=[pl.BlockSpec((4, 1, 26, 8, 128), lambda i: (i & 7, i >> 3, 0, 0, 0))],
        out_specs=(
            pl.BlockSpec((WIDTH, 256), lambda i: (0, i)),
            pl.BlockSpec((RELGROUPS, 128), lambda i: (0, 0)),
        ),
        out_shape=(
            jax.ShapeDtypeStruct((WIDTH, REL), F32),
            jax.ShapeDtypeStruct((RELGROUPS, 128), F32),
        ),
        compiler_params=pltpu.CompilerParams(vmem_limit_bytes=VMEM_LIMIT),
        name="unpack",
    )(shards)


def exchange(x, axis):
    return lax.all_to_all(x, axis, split_axis=0, concat_axis=0, tiled=True)


def any_device(flag):
    largest = flag
    for k in (1, 2, 3):
        moved = lax.ppermute(flag, "rep", [(p, (p + k) % 4) for p in range(4)])
        largest = jnp.maximum(largest, moved)
    return largest


def per_device(
    entity_table,
    entity_state,
    relation_table,
    relation_state,
    end_owner,
    end_row,
    relation_id,
    negative_owner,
    negative_row,
):
    table_t = entity_table.T
    to_right = [(p, (p + 1) % 4) for p in range(4)]
    to_left = [(p, (p + 3) % 4) for p in range(4)]
    left = lax.ppermute(table_t, "rep", to_right)
    right = lax.ppermute(table_t, "rep", to_left)
    across_a = lax.ppermute(left[: WIDTH // 2], "rep", to_right)
    across_b = lax.ppermute(right[WIDTH // 2 :], "rep", to_left)
    tables = (table_t, right, across_a, across_b, left)
    rows_at, rep_at = lax.axis_index("rows"), lax.axis_index("rep")
    request, addr = prep(
        rep_at.reshape(1),
        end_owner.T, end_row.T, negative_owner.reshape(1, NEG), negative_row.reshape(8, 128)
    )
    wanted = exchange(request.reshape(GROUP, 2, 128), "rows")
    wanted_rows = wanted.reshape(2 * GROUP, 128)
    looked = lookup(MAIN, 0, wanted_rows, tables)
    arrived = exchange(looked, "rows")
    flag = any_device(jnp.max(wanted[:, 1, FLAG]).reshape(1))
    over_now = flag[0] > 0
    rel_rows = jnp.pad(relation_table[relation_id], ((0, 0), (0, 112)))
    grads, rel_grads = lax.cond(
        over_now,
        lambda x: math(
            addr, flag, x, exchange(lookup(OVER, MAIN, wanted_rows, tables), "rows"), rel_rows
        ),
        lambda x: math(addr, flag, x, x, rel_rows),
        arrived,
    )
    relation_grad = relation_sum(relation_id.reshape(8, 128), rel_grads)
    grads, relation_grad = lax.optimization_barrier((grads, relation_grad))
    part_grad = lax.psum_scatter(
        relation_grad.reshape(4, GROUP, 25, 8, 128), "rep", scatter_dimension=0, tiled=True
    )
    outgoing, outgoing_over = pack_grads(addr, flag, grads)
    incoming = exchange(outgoing, "rows")
    incoming, part_grad = lax.optimization_barrier((incoming, part_grad))
    shard_grad = lax.psum_scatter(
        part_grad.reshape(GROUP, 25, 8, 128), "rows", scatter_dimension=0, tiled=True
    )
    slots = wanted.reshape(GROUP, 256)

    def ids(first, octets):
        part = slots[:, first * 8 : (first + octets) * 8]
        return part.reshape(GROUP // SUM_STEP, 1, SUM_STEP * octets * 8)

    summed = row_sum(MAIN, ids(0, MAIN), incoming)
    summed, shard_grad = lax.optimization_barrier((summed, shard_grad))
    summed = lax.cond(
        over_now,
        lambda x: x + row_sum(OVER, ids(MAIN, OVER), exchange(outgoing_over, "rows")),
        lambda x: x,
        summed,
    )
    entity_grads = exchange(jnp.roll(summed, rep_at, axis=0), "rep")
    new_entity_table, new_entity_state = entity_update(
        entity_grads, table_t, entity_state.reshape(1, ENT)
    )
    new_shard = relation_update(
        (rep_at * GROUP + rows_at).reshape(1),
        shard_grad.reshape(25, 8, 128),
        relation_table.T,
        relation_state.reshape(RELGROUPS, 128),
    )
    shards = lax.all_gather(new_shard, AXES, axis=0, tiled=False)
    new_relation_table, new_relation_state = unpack(shards.reshape(GROUP, 4, 26, 8, 128))
    return (
        new_entity_table.T,
        new_entity_state.reshape(ENT),
        new_relation_table.T,
        new_relation_state.reshape(REL),
    )


def solution(mesh):
    return jax.shard_map(
        per_device,
        mesh=mesh,
        in_specs=(
            P(AXES, None),
            P(AXES),
            P(),
            P(),
            P(AXES, None),
            P(AXES, None),
            P(AXES),
            P(AXES, None),
            P(AXES),
        ),
        out_specs=(P(AXES, None), P(AXES), P(), P()),
        check_vma=False,
    )
```

```python
import functools
import jax
import jax.numpy as jnp
from jax import lax
from jax.experimental import pallas as pl
from jax.experimental.pallas import tpu as pltpu
from jax.sharding import PartitionSpec as P


learn_rate = 0.5
adagrad_eps = 1e-10

AXES = ("rows", "rep")
F32, BF16, I32 = jnp.float32, jnp.bfloat16, jnp.int32
ENT = 512
WIDTH = 400
EDGE = 1024
NEG = 1024
GROUP = 32
MAIN = 24
OCT = 28
OVER = OCT - MAIN
MAIN_TILES = 3 * MAIN + 3
OVER_TILES = 3 * OVER + 1
REL = 7424
RELGROUPS = REL // 128
SHARDS = 64
VMEM_LIMIT = 60 * 1024 * 1024
FLAG = 127
COUNT = 126


def dot(a, b, dims):
    return lax.dot_general(a, b, (dims, ((), ())), preferred_element_type=F32)


NN = ((1,), (0,))
NT = ((1,), (1,))
TN = ((0,), (0,))


def split(x):
    hi = x.astype(BF16)
    return hi, (x - hi.astype(F32)).astype(BF16)


def prep_kernel(me_ref, end_owner, end_row, neg_owner, neg_row, request_ref, addr_ref):
    iota0 = lax.broadcasted_iota(I32, (128, 128), 0)
    upper = (iota0 < lax.broadcasted_iota(I32, (128, 128), 1)).astype(BF16)
    group = lax.broadcasted_iota(I32, (GROUP, 128), 0)
    double = lax.broadcasted_iota(I32, (2 * GROUP, 128), 0)
    count = jnp.zeros((GROUP, 1), F32)
    low = jnp.zeros((2 * GROUP, 128), F32)
    high = jnp.zeros((2 * GROUP, 128), F32)
    for i in range(24):
        lanes = slice((i & 7) * 128, (i & 7) * 128 + 128)
        if i < 16:
            owner = end_owner[i >> 3 : (i >> 3) + 1, lanes]
            row = end_row[i >> 3 : (i >> 3) + 1, lanes]
        else:
            owner = neg_owner[:, lanes]
            row = neg_row[i - 16 : i - 15, :]
        target = owner >> 2
        near = (owner - me_ref[0]) & 3
        value = near * (4 * ENT) + (row >> 3) * 32 + (row & 7)
        onehot = (group == target).astype(F32)
        earlier = dot(onehot.astype(BF16), upper, NN) + count
        rank = jnp.sum(onehot * earlier, axis=0, keepdims=True).astype(I32)
        count = count + jnp.sum(onehot, axis=1, keepdims=True)
        wide = (double == 2 * target + (rank >> 7)).astype(F32).astype(BF16)
        at = iota0 == (rank & 127)
        low = low + dot(wide, jnp.where(at, (value & 255).astype(F32), 0.0).astype(BF16), NT)
        high = high + dot(wide, jnp.where(at, (value >> 8).astype(F32), 0.0).astype(BF16), NT)
        addr_ref[i : i + 1, :] = (target * OCT + (rank >> 3)) * 32 + (rank & 7)
    most = jnp.max(count, axis=0, keepdims=True)
    flag = (most > 8.0 * MAIN).astype(F32)
    lane = lax.broadcasted_iota(I32, (2 * GROUP, 128), 1)
    mark = (lane == FLAG) & ((double & 1) == 1)
    pair = lax.broadcasted_iota(I32, (2 * GROUP, GROUP), 0) >> 1
    same = pair == lax.broadcasted_iota(I32, (2 * GROUP, GROUP), 1)
    half = (2.0 * jnp.floor(count * 0.5), count)
    low_count = half[1] - half[0]
    counts = dot(same.astype(F32).astype(BF16), (half[0] * 0.5).astype(BF16), NN) * 2.0
    counts = counts + dot(same.astype(F32).astype(BF16), low_count.astype(BF16), NN)
    request = jnp.where(mark, flag, low + 256.0 * high)
    mark = (lane == COUNT) & ((double & 1) == 1)
    request_ref[...] = jnp.where(mark, counts, request).astype(I32)


def prep(me, end_owner, end_row, neg_owner, neg_row):
    return pl.pallas_call(
        prep_kernel,
        out_shape=(
            jax.ShapeDtypeStruct((2 * GROUP, 128), I32),
            jax.ShapeDtypeStruct((24, 128), I32),
        ),
        in_specs=[pl.BlockSpec(memory_space=pltpu.SMEM)]
        + [pl.BlockSpec(memory_space=pltpu.VMEM)] * 4,
        name="prep",
    )(me, end_owner, end_row, neg_owner, neg_row)


STEP = 4


def lookup_kernel(
    octets, first, wanted_ref, own, right, across_a, across_b, left, out_ref, table, rows
):
    step = pl.program_id(0)

    @pl.when(step == 0)
    def _():
        def turn(b, _):
            lanes = pl.ds(pl.multiple_of(b * 128, 128), 128)
            for i, parts in enumerate(((own,), (right,), (across_a, across_b), (left,))):
                height = WIDTH // len(parts)
                for t in range(4):
                    pieces, low, high = [], t * 128, min(t * 128 + 128, WIDTH)
                    for n, part in enumerate(parts):
                        start, stop = max(low, n * height), min(high, (n + 1) * height)
                        if start < stop:
                            pieces.append(part[start - n * height : stop - n * height, lanes])
                    if t == 3:
                        pieces.append(jnp.zeros((112, 128), F32))
                    block = pieces[0] if len(pieces) == 1 else jnp.concatenate(pieces, axis=0)
                    table[pl.ds(i * 64 + b * 16, 16), t] = block.T.reshape(16, 8, 128)
            return 0

        lax.fori_loop(0, 4, turn, 0)

    flat = table.reshape(256 * 32, 128)
    rows_flat = rows.reshape(STEP * octets * 32, 128)
    for d in range(STEP):
        g = step * STEP + d
        used = (wanted_ref[2 * g + 1, COUNT] + 7) >> 3
        used = jnp.clip(used - first, 0, octets)

        def fetch(q, _):
            k = (q + first) * 8
            line, lane = 2 * g + (k >> 7), k & 127
            for j in range(8):
                a = wanted_ref[line, lane + j]
                rows_flat[pl.ds((d * octets + q) * 32 + j, 4, stride=8), :] = flat[
                    pl.ds(a, 4, stride=8), :
                ]
            return 0

        lax.fori_loop(0, used, fetch, 0)

        def blank(q, _):
            rows[d, q, 3] = jnp.zeros((8, 128), F32)
            return 0

        lax.fori_loop(used, octets, blank, 0)
    for q in range(octets):
        out_ref[:, 3 * q : 3 * q + 3] = rows[:, q, 0:3]
    for tile in range((octets + 7) // 8):
        rest = rows[:, tile * 8, 3]
        for q in range(tile * 8 + 1, min(octets, tile * 8 + 8)):
            rest = rest + pltpu.roll(rows[:, q, 3], 16 * (q & 7), 2)
        out_ref[:, 3 * octets + tile] = rest


def lookup(octets, first, wanted, tables):
    tiles = 3 * octets + (octets + 7) // 8
    return pl.pallas_call(
        functools.partial(lookup_kernel, octets, first),
        grid=(GROUP // STEP,),
        in_specs=[pl.BlockSpec(memory_space=pltpu.SMEM)]
        + [pl.BlockSpec(x.shape, lambda i: (0, 0)) for x in tables],
        out_specs=pl.BlockSpec((STEP, tiles, 8, 128), lambda i: (i, 0, 0, 0)),
        out_shape=jax.ShapeDtypeStruct((GROUP, tiles, 8, 128), F32),
        scratch_shapes=[
            pltpu.VMEM((256, 4, 8, 128), F32),
            pltpu.VMEM((STEP, octets, 4, 8, 128), F32),
        ],
        compiler_params=pltpu.CompilerParams(vmem_limit_bytes=VMEM_LIMIT),
        name="lookup" if first == 0 else "lookup_over",
    )(wanted, *tables)


BLOCK = 256


def math_kernel(
    addr_ref, flag_ref, pay_ref, over_ref, rel_ref, grad_ref, rel_grad_ref,
    rows, rest, hr_hi, hr_lo, n_hi, n_lo, g_neg, sems,
):
    def fill(source, octets, first, tile, sem):
        copies = [
            pltpu.make_async_copy(
                source.at[:, 3 * q : 3 * q + 3], rows.at[:, first + q, 0:3], sems.at[sem + 1 + q]
            )
            for q in range(octets)
        ]
        tiles = (octets + 7) // 8
        last = pltpu.make_async_copy(
            source.at[:, 3 * octets : 3 * octets + tiles],
            rest.at[:, tile : tile + tiles],
            sems.at[sem],
        )
        last.start()
        for copy in copies:
            copy.start()
        last.wait()
        lane = lax.broadcasted_iota(I32, (8, 8, 128), 2)

        def expand(i, _):
            for q in range(octets):
                part = rest[pl.ds(i * 8, 8), tile + (q >> 3)]
                if q & 7:
                    part = pltpu.roll(part, 128 - 16 * (q & 7), 2)
                rows[pl.ds(i * 8, 8), first + q, 3] = jnp.where(lane < 16, part, 0.0)
            return 0

        lax.fori_loop(0, GROUP // 8, expand, 0)
        for copy in copies:
            copy.wait()

    fill(pay_ref, MAIN, 0, 0, 0)

    @pl.when(flag_ref[0] > 0)
    def _():
        fill(over_ref, OVER, MAIN, 3, MAIN + 1)

    flat = rows.reshape(GROUP * OCT * 32, 128)
    grad_flat = grad_ref.reshape(384 * 32, 128)

    def gather(i, _):
        for j in range(8):
            a = addr_ref[i >> 4, (i & 15) * 8 + j]
            grad_flat[pl.ds(i * 32 + j, 4, stride=8), :] = flat[pl.ds(a, 4, stride=8), :]
        return 0

    lax.fori_loop(0, 384, gather, 0, unroll=4)

    def prepare(b, _):
        octets = pl.ds(b * 32, 32)
        edges = pl.ds(b * BLOCK, BLOCK)
        for t in range(4):
            lanes = slice(t * 128, (t + 1) * 128)
            hr = grad_ref[octets, t].reshape(BLOCK, 128) * rel_ref[edges, lanes]
            hr_hi[edges, lanes], hr_lo[edges, lanes] = split(hr)
            neg = grad_ref[pl.ds(256 + b * 32, 32), t].reshape(BLOCK, 128)
            n_hi[edges, lanes], n_lo[edges, lanes] = split(neg)
        return 0

    lax.fori_loop(0, EDGE // BLOCK, prepare, 0)
    g_neg[...] = jnp.zeros_like(g_neg)

    def block(b, _):
        edges = pl.ds(b * BLOCK, BLOCK)
        octets = pl.ds(b * 32, 32)
        tails = pl.ds(128 + b * 32, 32)
        a_hi, a_lo = hr_hi[edges, :], hr_lo[edges, :]
        score = dot(a_hi, n_hi[...], NT) + dot(a_hi, n_lo[...], NT) + dot(a_lo, n_hi[...], NT)
        p_hi, p_lo = split(1.0 / (1.0 + jnp.exp(-score)))
        g_hr = dot(p_hi, n_hi[...], NN) + dot(p_hi, n_lo[...], NN) + dot(p_lo, n_hi[...], NN)
        g_neg[...] += dot(p_hi, a_hi, TN) + dot(p_hi, a_lo, TN) + dot(p_lo, a_hi, TN)
        total = jnp.zeros((BLOCK, 128), F32)
        for t in range(4):
            lanes = slice(t * 128, (t + 1) * 128)
            hr = grad_ref[octets, t].reshape(BLOCK, 128) * rel_ref[edges, lanes]
            total = total + hr * grad_ref[tails, t].reshape(BLOCK, 128)
        positive = jnp.sum(total, axis=1, keepdims=True)
        d_pos = -1.0 / (1.0 + jnp.exp(positive))
        for t in range(4):
            lanes = slice(t * 128, (t + 1) * 128)
            head = grad_ref[octets, t].reshape(BLOCK, 128)
            tail = grad_ref[tails, t].reshape(BLOCK, 128)
            rel = rel_ref[edges, lanes]
            g = d_pos * tail + g_hr[:, lanes] * (1.0 / NEG)
            rel_grad_ref[octets, t] = (g * head).reshape(32, 8, 128)
            grad_ref[tails, t] = (d_pos * (head * rel)).reshape(32, 8, 128)
            grad_ref[octets, t] = (g * rel).reshape(32, 8, 128)
        return 0

    lax.fori_loop(0, EDGE // BLOCK, block, 0)
    for t in range(4):
        lanes = slice(t * 128, (t + 1) * 128)
        grad_ref[256:384, t] = (g_neg[:, lanes] * (1.0 / NEG)).reshape(128, 8, 128)


def math(addr, flag, arrived, over, rel_rows):
    return pl.pallas_call(
        math_kernel,
        in_specs=[
            pl.BlockSpec(memory_space=pltpu.SMEM),
            pl.BlockSpec(memory_space=pltpu.SMEM),
            pl.BlockSpec(memory_space=pl.ANY),
            pl.BlockSpec(memory_space=pl.ANY),
            pl.BlockSpec(memory_space=pltpu.VMEM),
        ],
        out_specs=(
            pl.BlockSpec(memory_space=pltpu.VMEM),
            pl.BlockSpec(memory_space=pltpu.VMEM),
        ),
        out_shape=(
            jax.ShapeDtypeStruct((384, 4, 8, 128), F32),
            jax.ShapeDtypeStruct((128, 4, 8, 128), F32),
        ),
        scratch_shapes=[
            pltpu.VMEM((GROUP, OCT, 4, 8, 128), F32),
            pltpu.VMEM((GROUP, 4, 8, 128), F32),
            pltpu.VMEM((EDGE, 512), BF16),
            pltpu.VMEM((EDGE, 512), BF16),
            pltpu.VMEM((NEG, 512), BF16),
            pltpu.VMEM((NEG, 512), BF16),
            pltpu.VMEM((NEG, 512), F32),
            pltpu.SemaphoreType.DMA((OCT + 2,)),
        ],
        compiler_params=pltpu.CompilerParams(vmem_limit_bytes=VMEM_LIMIT),
        name="math",
    )(addr, flag, arrived, over, rel_rows)


def relation_kernel(id_ref, other_id_ref, grad_ref, other_ref, out_ref, mine, others, packed, sems):
    zero = jnp.zeros((8, 4, 8, 128), F32)

    def clear(g, _):
        mine[pl.ds(g * 8, 8)] = zero
        others[pl.ds(g * 8, 8)] = zero
        return 0

    lax.fori_loop(0, SHARDS + 1, clear, 0)
    height = (SHARDS + 1) * 256
    sides = (
        (id_ref, grad_ref.reshape(128 * 32, 128), mine.reshape(height, 128)),
        (other_id_ref, other_ref.reshape(128 * 32, 128), others.reshape(height, 128)),
    )

    def add(i, _):
        for j in range(8):
            for ids, grad, flat in sides:
                at = pl.ds(ids[i >> 4, (i & 15) * 8 + j], 4, stride=8)
                flat[at, :] = flat[at, :] + grad[pl.ds(i * 32 + j, 4, stride=8), :]
        return 0

    lax.fori_loop(0, 128, add, 0)

    def copy(g):
        return pltpu.make_async_copy(
            packed.at[g & 1], out_ref.at[pl.ds(g * 4, 4)], sems.at[g & 1]
        )

    def pack(g, _):
        @pl.when(g >= 2)
        def _():
            copy(g - 2).wait()

        for n in range(4):
            first = g * 32 + n * 8
            for t in range(3):
                packed[g & 1, n, t * 8 : t * 8 + 8] = (
                    mine[pl.ds(first, 8), t] + others[pl.ds(first, 8), t]
                )
            rest = mine[first, 3] + others[first, 3]
            for q in range(1, 8):
                rest = rest + pltpu.roll(mine[first + q, 3] + others[first + q, 3], 16 * q, 1)
            packed[g & 1, n, 24] = rest
        copy(g).start()
        return 0

    lax.fori_loop(0, SHARDS // 4, pack, 0)
    copy(SHARDS // 4 - 2).wait()
    copy(SHARDS // 4 - 1).wait()


def relation_sum(ids, other_ids, grad, other):
    return pl.pallas_call(
        relation_kernel,
        in_specs=[
            pl.BlockSpec(memory_space=pltpu.SMEM),
            pl.BlockSpec(memory_space=pltpu.SMEM),
            pl.BlockSpec(memory_space=pltpu.VMEM),
            pl.BlockSpec(memory_space=pltpu.VMEM),
        ],
        out_specs=pl.BlockSpec(memory_space=pl.ANY),
        out_shape=jax.ShapeDtypeStruct((SHARDS, 25, 8, 128), F32),
        scratch_shapes=[
            pltpu.VMEM(((SHARDS + 1) * 8, 4, 8, 128), F32),
            pltpu.VMEM(((SHARDS + 1) * 8, 4, 8, 128), F32),
            pltpu.VMEM((2, 4, 25, 8, 128), F32),
            pltpu.SemaphoreType.DMA((2,)),
        ],
        compiler_params=pltpu.CompilerParams(vmem_limit_bytes=VMEM_LIMIT),
        name="relation_sum",
    )(ids, other_ids, grad, other)


def pack_kernel(addr_ref, flag_ref, grad_ref, out_ref, over_ref, rows, rest, sems):
    zero = jnp.zeros((2, OCT, 4, 8, 128), F32)

    def clear(i, _):
        rows[pl.ds(i * 2, 2)] = zero
        return 0

    lax.fori_loop(0, GROUP // 2, clear, 0)
    flat = rows.reshape(GROUP * OCT * 32, 128)
    grad_flat = grad_ref.reshape(384 * 32, 128)

    def scatter(i, _):
        for j in range(8):
            a = addr_ref[i >> 4, (i & 15) * 8 + j]
            flat[pl.ds(a, 4, stride=8), :] = grad_flat[pl.ds(i * 32 + j, 4, stride=8), :]
        return 0

    lax.fori_loop(0, 384, scatter, 0, unroll=4)

    def send(target, octets, first, tile, sem):
        copies = [
            pltpu.make_async_copy(
                rows.at[:, first + q, 0:3], target.at[:, 3 * q : 3 * q + 3], sems.at[sem + 1 + q]
            )
            for q in range(octets)
        ]
        for copy in copies:
            copy.start()
        tiles = (octets + 7) // 8

        def pack(i, _):
            at = pl.ds(i * 8, 8)
            for n in range(tiles):
                part = rows[at, first + n * 8, 3]
                for q in range(n * 8 + 1, min(octets, n * 8 + 8)):
                    part = part + pltpu.roll(rows[at, first + q, 3], 16 * (q & 7), 2)
                rest[at, tile + n] = part
            return 0

        lax.fori_loop(0, GROUP // 8, pack, 0)
        last = pltpu.make_async_copy(
            rest.at[:, tile : tile + tiles],
            target.at[:, 3 * octets : 3 * octets + tiles],
            sems.at[sem],
        )
        last.start()
        for copy in copies:
            copy.wait()
        last.wait()

    send(out_ref, MAIN, 0, 0, 0)

    @pl.when(flag_ref[0] > 0)
    def _():
        send(over_ref, OVER, MAIN, 3, MAIN + 1)


def pack_grads(addr, flag, grads):
    return pl.pallas_call(
        pack_kernel,
        in_specs=[
            pl.BlockSpec(memory_space=pltpu.SMEM),
            pl.BlockSpec(memory_space=pltpu.SMEM),
            pl.BlockSpec(memory_space=pltpu.VMEM),
        ],
        out_specs=(
            pl.BlockSpec(memory_space=pl.ANY),
            pl.BlockSpec(memory_space=pl.ANY),
        ),
        out_shape=(
            jax.ShapeDtypeStruct((GROUP, MAIN_TILES, 8, 128), F32),
            jax.ShapeDtypeStruct((GROUP, OVER_TILES, 8, 128), F32),
        ),
        scratch_shapes=[
            pltpu.VMEM((GROUP, OCT, 4, 8, 128), F32),
            pltpu.VMEM((GROUP, 4, 8, 128), F32),
            pltpu.SemaphoreType.DMA((OCT + 2,)),
        ],
        compiler_params=pltpu.CompilerParams(vmem_limit_bytes=VMEM_LIMIT),
        name="pack_grads",
    )(addr, flag, grads)


SUM_STEP = 8


def row_sum_kernel(octets, wanted_ref, pay_ref, out_ref, hi, lo, total):
    step = pl.program_id(0)
    slots = SUM_STEP * octets * 8

    @pl.when(step == 0)
    def _():
        total[...] = jnp.zeros_like(total)

    lane = lax.broadcasted_iota(I32, (SUM_STEP, 8, 128), 2)
    for t in range(4):
        lanes = slice(t * 128, (t + 1) * 128)
        parts = []
        for q in range(octets):
            if t < 3:
                parts.append(pay_ref[:, q * 3 + t])
            else:
                part = pay_ref[:, 3 * octets + (q >> 3)]
                if q & 7:
                    part = pltpu.roll(part, 128 - 16 * (q & 7), 2)
                parts.append(jnp.where(lane < 16, part, 0.0))
        hi[:, lanes], lo[:, lanes] = split(jnp.stack(parts, axis=1).reshape(slots, 128))
    wanted = wanted_ref[...].reshape(1, slots)

    def add(i, _):
        row = lax.broadcasted_iota(I32, (ENT, slots), 0)
        row = i * (4 * ENT) + (row >> 3) * 32 + (row & 7)
        onehot = (row == wanted).astype(F32).astype(BF16)
        total[i] = total[i] + (dot(onehot, hi[...], NN) + dot(onehot, lo[...], NN))
        return 0

    lax.fori_loop(0, 4, add, 0)

    @pl.when(step == pl.num_programs(0) - 1)
    def _():
        def turn(i, _):
            out_ref[i] = total[i].T[:WIDTH, :]
            return 0

        lax.fori_loop(0, 4, turn, 0)


def row_sum(octets, wanted, arrived):
    tiles = 3 * octets + (octets + 7) // 8
    slots = SUM_STEP * octets * 8
    return pl.pallas_call(
        functools.partial(row_sum_kernel, octets),
        grid=(GROUP // SUM_STEP,),
        in_specs=[
            pl.BlockSpec((1, 1, slots), lambda i: (i, 0, 0)),
            pl.BlockSpec((SUM_STEP, tiles, 8, 128), lambda i: (i, 0, 0, 0)),
        ],
        out_specs=pl.BlockSpec((4, WIDTH, ENT), lambda i: (0, 0, 0)),
        out_shape=jax.ShapeDtypeStruct((4, WIDTH, ENT), F32),
        scratch_shapes=[
            pltpu.VMEM((slots, 512), BF16),
            pltpu.VMEM((slots, 512), BF16),
            pltpu.VMEM((4, ENT, 512), F32),
        ],
        compiler_params=pltpu.CompilerParams(vmem_limit_bytes=VMEM_LIMIT),
        name="row_sum" if octets == MAIN else "row_sum_over",
    )(wanted, arrived)


def entity_kernel(grad_ref, table_ref, state_ref, new_table, new_state):
    grad = (grad_ref[0] + grad_ref[1]) + (grad_ref[2] + grad_ref[3])
    state = state_ref[...] + jnp.sum(grad * grad, axis=0, keepdims=True) / float(WIDTH)
    new_state[...] = state
    new_table[...] = table_ref[...] - learn_rate * grad / (jnp.sqrt(state) + adagrad_eps)


def entity_update(grads, table_t, state):
    return pl.pallas_call(
        entity_kernel,
        out_shape=(
            jax.ShapeDtypeStruct((WIDTH, ENT), F32),
            jax.ShapeDtypeStruct((1, ENT), F32),
        ),
        compiler_params=pltpu.CompilerParams(vmem_limit_bytes=VMEM_LIMIT),
        name="entity_update",
    )(grads, table_t, state)


def relation_update_kernel(shard_ref, parts_ref, table_ref, state_ref, out_ref, table, sem):
    shard = shard_ref[0]
    group = jnp.minimum(shard >> 1, RELGROUPS - 1)
    lanes = pl.ds(pl.multiple_of(group * 128, 128), 128)
    copy = pltpu.make_async_copy(table_ref.at[:, lanes], table, sem)
    copy.start()
    odd = (shard & 1) == 1

    def total(i, carry):
        return carry + parts_ref[i]

    packed = lax.fori_loop(1, 16, total, parts_ref[0])
    blank = jnp.zeros((64, 128), F32)
    parts = []
    for t in range(4):
        if t < 3:
            part = packed[t * 8 : t * 8 + 8].reshape(64, 128)
        else:
            rest = packed[24]
            part = jnp.concatenate(
                [rest] + [pltpu.roll(rest, 128 - 16 * q, 1) for q in range(1, 8)], axis=0
            )
        both = jnp.concatenate(
            [jnp.where(odd, 0.0, part), jnp.where(odd, part, 0.0)], axis=0
        ).T
        parts.append(both if t < 3 else both[:16])
    grad = jnp.concatenate(parts, axis=0)
    state = state_ref[pl.ds(group, 1), :]
    state = state + jnp.sum(grad * grad, axis=0, keepdims=True) / float(WIDTH)
    copy.wait()
    new = table[...] - grad * (learn_rate / (jnp.sqrt(state) + adagrad_eps))
    top, bottom = new[: WIDTH // 2], new[WIDTH // 2 :]
    low = lax.broadcasted_iota(I32, (WIDTH // 2, 128), 1) < 64
    even_rows = jnp.where(low, top, pltpu.roll(bottom, 64, 1))
    odd_rows = jnp.where(low, pltpu.roll(top, 64, 1), bottom)
    out_ref[0:25] = jnp.where(odd, odd_rows, even_rows).reshape(25, 8, 128)
    out_ref[25] = jnp.broadcast_to(state, (8, 128))


def relation_update(shard, grad, table_t, state):
    return pl.pallas_call(
        relation_update_kernel,
        in_specs=[
            pl.BlockSpec(memory_space=pltpu.SMEM),
            pl.BlockSpec(memory_space=pltpu.VMEM),
            pl.BlockSpec(memory_space=pl.ANY),
            pl.BlockSpec(memory_space=pltpu.VMEM),
        ],
        out_specs=pl.BlockSpec(memory_space=pltpu.VMEM),
        out_shape=jax.ShapeDtypeStruct((26, 8, 128), F32),
        scratch_shapes=[pltpu.VMEM((WIDTH, 128), F32), pltpu.SemaphoreType.DMA],
        compiler_params=pltpu.CompilerParams(vmem_limit_bytes=VMEM_LIMIT),
        name="relation_update",
    )(shard, grad, table_t, state)


def unpack_kernel(shards_ref, new_table, new_state):
    low = lax.broadcasted_iota(I32, (WIDTH // 2, 128), 1) < 64
    for g in range(4):
        lanes = slice(g * 128, (g + 1) * 128)
        even = shards_ref[2 * g, 0, 0, 0:25].reshape(WIDTH // 2, 128)
        odd = shards_ref[2 * g + 1, 0, 0, 0:25].reshape(WIDTH // 2, 128)
        new_table[: WIDTH // 2, lanes] = jnp.where(low, even, pltpu.roll(odd, 64, 1))
        new_table[WIDTH // 2 :, lanes] = jnp.where(low, pltpu.roll(even, 64, 1), odd)
        state = jnp.where(low[:8], shards_ref[2 * g, 0, 0, 25], shards_ref[2 * g + 1, 0, 0, 25])
        group = pl.program_id(0) * 4 + g

        @pl.when(group < RELGROUPS)
        def _():
            new_state[pl.ds(group, 1), :] = state[0:1]


def unpack(shards):
    return pl.pallas_call(
        unpack_kernel,
        grid=(pl.cdiv(RELGROUPS, 4),),
        in_specs=[
            pl.BlockSpec(
                (8, 1, 1, 26, 8, 128), lambda i: (i & 1, i >> 3, (i >> 1) & 3, 0, 0, 0)
            )
        ],
        out_specs=(
            pl.BlockSpec((WIDTH, 512), lambda i: (0, i)),
            pl.BlockSpec((RELGROUPS, 128), lambda i: (0, 0)),
        ),
        out_shape=(
            jax.ShapeDtypeStruct((WIDTH, REL), F32),
            jax.ShapeDtypeStruct((RELGROUPS, 128), F32),
        ),
        compiler_params=pltpu.CompilerParams(vmem_limit_bytes=VMEM_LIMIT),
        name="unpack",
    )(shards)


def exchange(x, axis, groups=None):
    return lax.all_to_all(
        x, axis, split_axis=0, concat_axis=0, tiled=True, axis_index_groups=groups
    )


def any_device(flag):
    largest = flag
    for k in (1, 2, 3):
        moved = lax.ppermute(flag, "rep", [(p, (p + k) % 4) for p in range(4)])
        largest = jnp.maximum(largest, moved)
    return largest


def per_device(
    entity_table,
    entity_state,
    relation_table,
    relation_state,
    end_owner,
    end_row,
    relation_id,
    negative_owner,
    negative_row,
):
    table_t = entity_table.T
    to_right = [(p, (p + 1) % 4) for p in range(4)]
    to_left = [(p, (p + 3) % 4) for p in range(4)]
    left = lax.ppermute(table_t, "rep", to_right)
    right = lax.ppermute(table_t, "rep", to_left)
    rows_at, rep_at = lax.axis_index("rows"), lax.axis_index("rep")
    request, addr = prep(
        rep_at.reshape(1),
        end_owner.T, end_row.T, negative_owner.reshape(1, NEG), negative_row.reshape(8, 128)
    )
    wanted = exchange(request.reshape(GROUP, 2, 128), "rows")
    left, right, _ = lax.optimization_barrier((left, right, wanted))
    across_a = lax.ppermute(left[: WIDTH // 2], "rep", to_right)
    across_b = lax.ppermute(right[WIDTH // 2 :], "rep", to_left)
    tables = (table_t, right, across_a, across_b, left)
    wanted_rows = wanted.reshape(2 * GROUP, 128)
    looked = lookup(MAIN, 0, wanted_rows, tables)
    arrived = exchange(looked, "rows")
    flag = any_device(jnp.max(wanted[:, 1, FLAG]).reshape(1))
    over_now = flag[0] > 0
    rel_rows = jnp.pad(relation_table[relation_id], ((0, 0), (0, 112)))
    grads, rel_grads = lax.cond(
        over_now,
        lambda x: math(
            addr, flag, x, exchange(lookup(OVER, MAIN, wanted_rows, tables), "rows"), rel_rows
        ),
        lambda x: math(addr, flag, x, x, rel_rows),
        arrived,
    )
    core, twins = rows_at & 1, [[r for r in range(GROUP) if r % 2 == c] for c in (0, 1)]
    swap = [(r, r ^ 1) for r in range(GROUP)]
    other_id = lax.ppermute(relation_id, "rows", swap)
    other_grads = lax.ppermute(rel_grads, "rows", swap)

    def places(ids):
        near = ids - core * (SHARDS * 64)
        near = jnp.where((near >= 0) & (near < SHARDS * 64), near, SHARDS * 64)
        return ((near >> 3) * 32 + (near & 7)).reshape(8, 128)

    outgoing, outgoing_over = pack_grads(addr, flag, grads)
    incoming = exchange(outgoing, "rows")
    rel_grads, other_grads, _ = lax.optimization_barrier((rel_grads, other_grads, outgoing))
    relation_grad = relation_sum(
        places(relation_id), places(other_id), rel_grads, other_grads
    )
    part_grad = lax.psum_scatter(
        relation_grad.reshape(4, 16, 25, 8, 128), "rep", scatter_dimension=0, tiled=True
    )
    incoming, part_grad = lax.optimization_barrier((incoming, part_grad))
    shard_grads = exchange(part_grad.reshape(16, 25, 8, 128), "rows", twins)
    slots = wanted.reshape(GROUP, 256)

    def ids(first, octets):
        part = slots[:, first * 8 : (first + octets) * 8]
        return part.reshape(GROUP // SUM_STEP, 1, SUM_STEP * octets * 8)

    summed = row_sum(MAIN, ids(0, MAIN), incoming)
    summed, shard_grads = lax.optimization_barrier((summed, shard_grads))
    summed = lax.cond(
        over_now,
        lambda x: x + row_sum(OVER, ids(MAIN, OVER), exchange(outgoing_over, "rows")),
        lambda x: x,
        summed,
    )
    entity_grads = exchange(jnp.roll(summed, rep_at, axis=0), "rep")
    new_entity_table, new_entity_state = entity_update(
        entity_grads, table_t, entity_state.reshape(1, ENT)
    )
    new_shard = relation_update(
        (core * SHARDS + rep_at * 16 + (rows_at >> 1)).reshape(1),
        shard_grads,
        relation_table.T,
        relation_state.reshape(RELGROUPS, 128),
    )
    shards = lax.all_gather(new_shard, AXES, axis=0, tiled=False)
    new_relation_table, new_relation_state = unpack(shards.reshape(16, 2, 4, 26, 8, 128))
    return (
        new_entity_table.T,
        new_entity_state.reshape(ENT),
        new_relation_table.T,
        new_relation_state.reshape(REL),
    )


def solution(mesh):
    return jax.shard_map(
        per_device,
        mesh=mesh,
        in_specs=(
            P(AXES, None),
            P(AXES),
            P(),
            P(),
            P(AXES, None),
            P(AXES, None),
            P(AXES),
            P(AXES, None),
            P(AXES),
        ),
        out_specs=(P(AXES, None), P(AXES), P(), P()),
        check_vma=False,
    )
```

```python
import functools
import jax
import jax.numpy as jnp
from jax import lax
from jax.experimental import pallas as pl
from jax.experimental.pallas import tpu as pltpu
from jax.sharding import PartitionSpec as P


learn_rate = 0.5
adagrad_eps = 1e-10

AXES = ("rows", "rep")
F32, BF16, I32 = jnp.float32, jnp.bfloat16, jnp.int32
ENT = 512
WIDTH = 400
EDGE = 1024
NEG = 1024
GROUP = 32
MAIN = 23
OCT = 28
OVER = OCT - MAIN
MAIN_TILES = 3 * MAIN + 3
OVER_TILES = 3 * OVER + 1
REL = 7424
RELGROUPS = REL // 128
SHARDS = 64
VMEM_LIMIT = 60 * 1024 * 1024
FLAG = 127
COUNT = 126


def dot(a, b, dims):
    return lax.dot_general(a, b, (dims, ((), ())), preferred_element_type=F32)


NN = ((1,), (0,))
NT = ((1,), (1,))
TN = ((0,), (0,))


def split(x):
    hi = x.astype(BF16)
    return hi, (x - hi.astype(F32)).astype(BF16)


def prep_kernel(me_ref, end_owner, end_row, neg_owner, neg_row, request_ref, addr_ref):
    iota0 = lax.broadcasted_iota(I32, (128, 128), 0)
    upper = (iota0 < lax.broadcasted_iota(I32, (128, 128), 1)).astype(BF16)
    group = lax.broadcasted_iota(I32, (GROUP, 128), 0)
    double = lax.broadcasted_iota(I32, (2 * GROUP, 128), 0)
    count = jnp.zeros((GROUP, 1), F32)
    low = jnp.zeros((2 * GROUP, 128), F32)
    high = jnp.zeros((2 * GROUP, 128), F32)
    for i in range(24):
        lanes = slice((i & 7) * 128, (i & 7) * 128 + 128)
        if i < 16:
            owner = end_owner[i >> 3 : (i >> 3) + 1, lanes]
            row = end_row[i >> 3 : (i >> 3) + 1, lanes]
        else:
            owner = neg_owner[:, lanes]
            row = neg_row[i - 16 : i - 15, :]
        target = owner >> 2
        near = (owner - me_ref[0]) & 3
        value = near * (4 * ENT) + (row >> 3) * 32 + (row & 7)
        onehot = (group == target).astype(F32)
        earlier = dot(onehot.astype(BF16), upper, NN) + count
        rank = jnp.sum(onehot * earlier, axis=0, keepdims=True).astype(I32)
        count = count + jnp.sum(onehot, axis=1, keepdims=True)
        wide = (double == 2 * target + (rank >> 7)).astype(F32).astype(BF16)
        at = iota0 == (rank & 127)
        low = low + dot(wide, jnp.where(at, (value & 255).astype(F32), 0.0).astype(BF16), NT)
        high = high + dot(wide, jnp.where(at, (value >> 8).astype(F32), 0.0).astype(BF16), NT)
        addr_ref[i : i + 1, :] = (target * OCT + (rank >> 3)) * 32 + (rank & 7)
    most = jnp.max(count, axis=0, keepdims=True)
    flag = (most > 8.0 * MAIN).astype(F32)
    lane = lax.broadcasted_iota(I32, (2 * GROUP, 128), 1)
    mark = (lane == FLAG) & ((double & 1) == 1)
    pair = lax.broadcasted_iota(I32, (2 * GROUP, GROUP), 0) >> 1
    same = pair == lax.broadcasted_iota(I32, (2 * GROUP, GROUP), 1)
    half = (2.0 * jnp.floor(count * 0.5), count)
    low_count = half[1] - half[0]
    counts = dot(same.astype(F32).astype(BF16), (half[0] * 0.5).astype(BF16), NN) * 2.0
    counts = counts + dot(same.astype(F32).astype(BF16), low_count.astype(BF16), NN)
    request = jnp.where(mark, flag, low + 256.0 * high)
    mark = (lane == COUNT) & ((double & 1) == 1)
    request_ref[...] = jnp.where(mark, counts, request).astype(I32)


def prep(me, end_owner, end_row, neg_owner, neg_row):
    return pl.pallas_call(
        prep_kernel,
        out_shape=(
            jax.ShapeDtypeStruct((2 * GROUP, 128), I32),
            jax.ShapeDtypeStruct((24, 128), I32),
        ),
        in_specs=[pl.BlockSpec(memory_space=pltpu.SMEM)]
        + [pl.BlockSpec(memory_space=pltpu.VMEM)] * 4,
        name="prep",
    )(me, end_owner, end_row, neg_owner, neg_row)


STEP = 4


def lookup_kernel(
    octets, first, wanted_ref, own, right, across_a, across_b, left, out_ref, table, rows
):
    step = pl.program_id(0)

    @pl.when(step == 0)
    def _():
        def turn(b, _):
            lanes = pl.ds(pl.multiple_of(b * 128, 128), 128)
            for i, parts in enumerate(((own,), (right,), (across_a, across_b), (left,))):
                height = WIDTH // len(parts)
                for t in range(4):
                    pieces, low, high = [], t * 128, min(t * 128 + 128, WIDTH)
                    for n, part in enumerate(parts):
                        start, stop = max(low, n * height), min(high, (n + 1) * height)
                        if start < stop:
                            pieces.append(part[start - n * height : stop - n * height, lanes])
                    if t == 3:
                        pieces.append(jnp.zeros((112, 128), F32))
                    block = pieces[0] if len(pieces) == 1 else jnp.concatenate(pieces, axis=0)
                    table[pl.ds(i * 64 + b * 16, 16), t] = block.T.reshape(16, 8, 128)
            return 0

        lax.fori_loop(0, 4, turn, 0)

    flat = table.reshape(256 * 32, 128)
    rows_flat = rows.reshape(STEP * octets * 32, 128)
    for d in range(STEP):
        g = step * STEP + d
        used = (wanted_ref[2 * g + 1, COUNT] + 7) >> 3
        used = jnp.clip(used - first, 0, octets)

        def fetch(q, _):
            k = (q + first) * 8
            line, lane = 2 * g + (k >> 7), k & 127
            for j in range(8):
                a = wanted_ref[line, lane + j]
                rows_flat[pl.ds((d * octets + q) * 32 + j, 4, stride=8), :] = flat[
                    pl.ds(a, 4, stride=8), :
                ]
            return 0

        lax.fori_loop(0, used, fetch, 0)

        def blank(q, _):
            rows[d, q, 3] = jnp.zeros((8, 128), F32)
            return 0

        lax.fori_loop(used, octets, blank, 0)
    for q in range(octets):
        out_ref[:, 3 * q : 3 * q + 3] = rows[:, q, 0:3]
    for tile in range((octets + 7) // 8):
        rest = rows[:, tile * 8, 3]
        for q in range(tile * 8 + 1, min(octets, tile * 8 + 8)):
            rest = rest + pltpu.roll(rows[:, q, 3], 16 * (q & 7), 2)
        out_ref[:, 3 * octets + tile] = rest


def lookup(octets, first, wanted, tables):
    tiles = 3 * octets + (octets + 7) // 8
    return pl.pallas_call(
        functools.partial(lookup_kernel, octets, first),
        grid=(GROUP // STEP,),
        in_specs=[pl.BlockSpec(memory_space=pltpu.SMEM)]
        + [pl.BlockSpec(x.shape, lambda i: (0, 0)) for x in tables],
        out_specs=pl.BlockSpec((STEP, tiles, 8, 128), lambda i: (i, 0, 0, 0)),
        out_shape=jax.ShapeDtypeStruct((GROUP, tiles, 8, 128), F32),
        scratch_shapes=[
            pltpu.VMEM((256, 4, 8, 128), F32),
            pltpu.VMEM((STEP, octets, 4, 8, 128), F32),
        ],
        compiler_params=pltpu.CompilerParams(vmem_limit_bytes=VMEM_LIMIT),
        name="lookup" if first == 0 else "lookup_over",
    )(wanted, *tables)


BLOCK = 256


def math_kernel(
    addr_ref, flag_ref, pay_ref, over_ref, rel_ref, grad_ref, rel_grad_ref,
    rows, rest, hr_hi, hr_lo, n_hi, n_lo, g_neg, sems,
):
    def fill(source, octets, first, tile, sem):
        copies = [
            pltpu.make_async_copy(
                source.at[:, 3 * q : 3 * q + 3], rows.at[:, first + q, 0:3], sems.at[sem + 1 + q]
            )
            for q in range(octets)
        ]
        tiles = (octets + 7) // 8
        last = pltpu.make_async_copy(
            source.at[:, 3 * octets : 3 * octets + tiles],
            rest.at[:, tile : tile + tiles],
            sems.at[sem],
        )
        last.start()
        for copy in copies:
            copy.start()
        last.wait()
        lane = lax.broadcasted_iota(I32, (8, 8, 128), 2)

        def expand(i, _):
            for q in range(octets):
                part = rest[pl.ds(i * 8, 8), tile + (q >> 3)]
                if q & 7:
                    part = pltpu.roll(part, 128 - 16 * (q & 7), 2)
                rows[pl.ds(i * 8, 8), first + q, 3] = jnp.where(lane < 16, part, 0.0)
            return 0

        lax.fori_loop(0, GROUP // 8, expand, 0)
        for copy in copies:
            copy.wait()

    fill(pay_ref, MAIN, 0, 0, 0)

    @pl.when(flag_ref[0] > 0)
    def _():
        fill(over_ref, OVER, MAIN, 3, MAIN + 1)

    flat = rows.reshape(GROUP * OCT * 32, 128)
    grad_flat = grad_ref.reshape(384 * 32, 128)

    def gather(i, _):
        for j in range(8):
            a = addr_ref[i >> 4, (i & 15) * 8 + j]
            grad_flat[pl.ds(i * 32 + j, 4, stride=8), :] = flat[pl.ds(a, 4, stride=8), :]
        return 0

    lax.fori_loop(0, 384, gather, 0, unroll=4)

    def prepare(b, _):
        octets = pl.ds(b * 32, 32)
        edges = pl.ds(b * BLOCK, BLOCK)
        for t in range(4):
            lanes = slice(t * 128, (t + 1) * 128)
            hr = grad_ref[octets, t].reshape(BLOCK, 128) * rel_ref[edges, lanes]
            hr_hi[edges, lanes], hr_lo[edges, lanes] = split(hr)
            neg = grad_ref[pl.ds(256 + b * 32, 32), t].reshape(BLOCK, 128)
            n_hi[edges, lanes], n_lo[edges, lanes] = split(neg)
        return 0

    lax.fori_loop(0, EDGE // BLOCK, prepare, 0)
    g_neg[...] = jnp.zeros_like(g_neg)

    def block(b, _):
        edges = pl.ds(b * BLOCK, BLOCK)
        octets = pl.ds(b * 32, 32)
        tails = pl.ds(128 + b * 32, 32)
        a_hi, a_lo = hr_hi[edges, :], hr_lo[edges, :]
        score = dot(a_hi, n_hi[...], NT) + dot(a_hi, n_lo[...], NT) + dot(a_lo, n_hi[...], NT)
        p_hi, p_lo = split(1.0 / (1.0 + jnp.exp(-score)))
        g_hr = dot(p_hi, n_hi[...], NN) + dot(p_hi, n_lo[...], NN) + dot(p_lo, n_hi[...], NN)
        g_neg[...] += dot(p_hi, a_hi, TN) + dot(p_hi, a_lo, TN) + dot(p_lo, a_hi, TN)
        total = jnp.zeros((BLOCK, 128), F32)
        for t in range(4):
            lanes = slice(t * 128, (t + 1) * 128)
            hr = grad_ref[octets, t].reshape(BLOCK, 128) * rel_ref[edges, lanes]
            total = total + hr * grad_ref[tails, t].reshape(BLOCK, 128)
        positive = jnp.sum(total, axis=1, keepdims=True)
        d_pos = -1.0 / (1.0 + jnp.exp(positive))
        for t in range(4):
            lanes = slice(t * 128, (t + 1) * 128)
            head = grad_ref[octets, t].reshape(BLOCK, 128)
            tail = grad_ref[tails, t].reshape(BLOCK, 128)
            rel = rel_ref[edges, lanes]
            g = d_pos * tail + g_hr[:, lanes] * (1.0 / NEG)
            rel_grad_ref[octets, t] = (g * head).reshape(32, 8, 128)
            grad_ref[tails, t] = (d_pos * (head * rel)).reshape(32, 8, 128)
            grad_ref[octets, t] = (g * rel).reshape(32, 8, 128)
        return 0

    lax.fori_loop(0, EDGE // BLOCK, block, 0)
    for t in range(4):
        lanes = slice(t * 128, (t + 1) * 128)
        grad_ref[256:384, t] = (g_neg[:, lanes] * (1.0 / NEG)).reshape(128, 8, 128)


def math(addr, flag, arrived, over, rel_rows):
    return pl.pallas_call(
        math_kernel,
        in_specs=[
            pl.BlockSpec(memory_space=pltpu.SMEM),
            pl.BlockSpec(memory_space=pltpu.SMEM),
            pl.BlockSpec(memory_space=pl.ANY),
            pl.BlockSpec(memory_space=pl.ANY),
            pl.BlockSpec(memory_space=pltpu.VMEM),
        ],
        out_specs=(
            pl.BlockSpec(memory_space=pltpu.VMEM),
            pl.BlockSpec(memory_space=pltpu.VMEM),
        ),
        out_shape=(
            jax.ShapeDtypeStruct((384, 4, 8, 128), F32),
            jax.ShapeDtypeStruct((128, 4, 8, 128), F32),
        ),
        scratch_shapes=[
            pltpu.VMEM((GROUP, OCT, 4, 8, 128), F32),
            pltpu.VMEM((GROUP, 4, 8, 128), F32),
            pltpu.VMEM((EDGE, 512), BF16),
            pltpu.VMEM((EDGE, 512), BF16),
            pltpu.VMEM((NEG, 512), BF16),
            pltpu.VMEM((NEG, 512), BF16),
            pltpu.VMEM((NEG, 512), F32),
            pltpu.SemaphoreType.DMA((OCT + 2,)),
        ],
        compiler_params=pltpu.CompilerParams(vmem_limit_bytes=VMEM_LIMIT),
        name="math",
    )(addr, flag, arrived, over, rel_rows)


def relation_kernel(id_ref, other_id_ref, grad_ref, other_ref, out_ref, mine, others, packed, sems):
    zero = jnp.zeros((8, 4, 8, 128), F32)

    def clear(g, _):
        mine[pl.ds(g * 8, 8)] = zero
        others[pl.ds(g * 8, 8)] = zero
        return 0

    lax.fori_loop(0, SHARDS + 1, clear, 0)
    height = (SHARDS + 1) * 256
    sides = (
        (id_ref, grad_ref.reshape(128 * 32, 128), mine.reshape(height, 128)),
        (other_id_ref, other_ref.reshape(128 * 32, 128), others.reshape(height, 128)),
    )

    def add(i, _):
        for j in range(8):
            for ids, grad, flat in sides:
                at = pl.ds(ids[i >> 4, (i & 15) * 8 + j], 4, stride=8)
                flat[at, :] = flat[at, :] + grad[pl.ds(i * 32 + j, 4, stride=8), :]
        return 0

    lax.fori_loop(0, 128, add, 0)

    def copy(g):
        return pltpu.make_async_copy(
            packed.at[g & 1], out_ref.at[pl.ds(g * 4, 4)], sems.at[g & 1]
        )

    def pack(g, _):
        @pl.when(g >= 2)
        def _():
            copy(g - 2).wait()

        for n in range(4):
            first = g * 32 + n * 8
            for t in range(3):
                packed[g & 1, n, t * 8 : t * 8 + 8] = (
                    mine[pl.ds(first, 8), t] + others[pl.ds(first, 8), t]
                )
            rest = mine[first, 3] + others[first, 3]
            for q in range(1, 8):
                rest = rest + pltpu.roll(mine[first + q, 3] + others[first + q, 3], 16 * q, 1)
            packed[g & 1, n, 24] = rest
        copy(g).start()
        return 0

    lax.fori_loop(0, SHARDS // 4, pack, 0)
    copy(SHARDS // 4 - 2).wait()
    copy(SHARDS // 4 - 1).wait()


def relation_sum(ids, other_ids, grad, other):
    return pl.pallas_call(
        relation_kernel,
        in_specs=[
            pl.BlockSpec(memory_space=pltpu.SMEM),
            pl.BlockSpec(memory_space=pltpu.SMEM),
            pl.BlockSpec(memory_space=pltpu.VMEM),
            pl.BlockSpec(memory_space=pltpu.VMEM),
        ],
        out_specs=pl.BlockSpec(memory_space=pl.ANY),
        out_shape=jax.ShapeDtypeStruct((SHARDS, 25, 8, 128), F32),
        scratch_shapes=[
            pltpu.VMEM(((SHARDS + 1) * 8, 4, 8, 128), F32),
            pltpu.VMEM(((SHARDS + 1) * 8, 4, 8, 128), F32),
            pltpu.VMEM((2, 4, 25, 8, 128), F32),
            pltpu.SemaphoreType.DMA((2,)),
        ],
        compiler_params=pltpu.CompilerParams(vmem_limit_bytes=VMEM_LIMIT),
        name="relation_sum",
    )(ids, other_ids, grad, other)


def pack_kernel(addr_ref, flag_ref, grad_ref, out_ref, over_ref, rows, rest, sems):
    zero = jnp.zeros((2, OCT, 4, 8, 128), F32)

    def clear(i, _):
        rows[pl.ds(i * 2, 2)] = zero
        return 0

    lax.fori_loop(0, GROUP // 2, clear, 0)
    flat = rows.reshape(GROUP * OCT * 32, 128)
    grad_flat = grad_ref.reshape(384 * 32, 128)

    def scatter(i, _):
        for j in range(8):
            a = addr_ref[i >> 4, (i & 15) * 8 + j]
            flat[pl.ds(a, 4, stride=8), :] = grad_flat[pl.ds(i * 32 + j, 4, stride=8), :]
        return 0

    lax.fori_loop(0, 384, scatter, 0, unroll=4)

    def send(target, octets, first, tile, sem):
        copies = [
            pltpu.make_async_copy(
                rows.at[:, first + q, 0:3], target.at[:, 3 * q : 3 * q + 3], sems.at[sem + 1 + q]
            )
            for q in range(octets)
        ]
        for copy in copies:
            copy.start()
        tiles = (octets + 7) // 8

        def pack(i, _):
            at = pl.ds(i * 8, 8)
            for n in range(tiles):
                part = rows[at, first + n * 8, 3]
                for q in range(n * 8 + 1, min(octets, n * 8 + 8)):
                    part = part + pltpu.roll(rows[at, first + q, 3], 16 * (q & 7), 2)
                rest[at, tile + n] = part
            return 0

        lax.fori_loop(0, GROUP // 8, pack, 0)
        last = pltpu.make_async_copy(
            rest.at[:, tile : tile + tiles],
            target.at[:, 3 * octets : 3 * octets + tiles],
            sems.at[sem],
        )
        last.start()
        for copy in copies:
            copy.wait()
        last.wait()

    send(out_ref, MAIN, 0, 0, 0)

    @pl.when(flag_ref[0] > 0)
    def _():
        send(over_ref, OVER, MAIN, 3, MAIN + 1)


def pack_grads(addr, flag, grads):
    return pl.pallas_call(
        pack_kernel,
        in_specs=[
            pl.BlockSpec(memory_space=pltpu.SMEM),
            pl.BlockSpec(memory_space=pltpu.SMEM),
            pl.BlockSpec(memory_space=pltpu.VMEM),
        ],
        out_specs=(
            pl.BlockSpec(memory_space=pl.ANY),
            pl.BlockSpec(memory_space=pl.ANY),
        ),
        out_shape=(
            jax.ShapeDtypeStruct((GROUP, MAIN_TILES, 8, 128), F32),
            jax.ShapeDtypeStruct((GROUP, OVER_TILES, 8, 128), F32),
        ),
        scratch_shapes=[
            pltpu.VMEM((GROUP, OCT, 4, 8, 128), F32),
            pltpu.VMEM((GROUP, 4, 8, 128), F32),
            pltpu.SemaphoreType.DMA((OCT + 2,)),
        ],
        compiler_params=pltpu.CompilerParams(vmem_limit_bytes=VMEM_LIMIT),
        name="pack_grads",
    )(addr, flag, grads)


SUM_STEP = 8


def row_sum_kernel(octets, wanted_ref, pay_ref, out_ref, hi, lo, total):
    step = pl.program_id(0)
    slots = SUM_STEP * octets * 8

    @pl.when(step == 0)
    def _():
        total[...] = jnp.zeros_like(total)

    lane = lax.broadcasted_iota(I32, (SUM_STEP, 8, 128), 2)
    for t in range(4):
        lanes = slice(t * 128, (t + 1) * 128)
        parts = []
        for q in range(octets):
            if t < 3:
                parts.append(pay_ref[:, q * 3 + t])
            else:
                part = pay_ref[:, 3 * octets + (q >> 3)]
                if q & 7:
                    part = pltpu.roll(part, 128 - 16 * (q & 7), 2)
                parts.append(jnp.where(lane < 16, part, 0.0))
        hi[:, lanes], lo[:, lanes] = split(jnp.stack(parts, axis=1).reshape(slots, 128))
    wanted = wanted_ref[...].reshape(1, slots)

    def add(i, _):
        row = lax.broadcasted_iota(I32, (ENT, slots), 0)
        row = i * (4 * ENT) + (row >> 3) * 32 + (row & 7)
        onehot = (row == wanted).astype(F32).astype(BF16)
        total[i] = total[i] + (dot(onehot, hi[...], NN) + dot(onehot, lo[...], NN))
        return 0

    lax.fori_loop(0, 4, add, 0)

    @pl.when(step == pl.num_programs(0) - 1)
    def _():
        def turn(i, _):
            out_ref[i] = total[i].T[:WIDTH, :]
            return 0

        lax.fori_loop(0, 4, turn, 0)


def row_sum(octets, wanted, arrived):
    tiles = 3 * octets + (octets + 7) // 8
    slots = SUM_STEP * octets * 8
    return pl.pallas_call(
        functools.partial(row_sum_kernel, octets),
        grid=(GROUP // SUM_STEP,),
        in_specs=[
            pl.BlockSpec((1, 1, slots), lambda i: (i, 0, 0)),
            pl.BlockSpec((SUM_STEP, tiles, 8, 128), lambda i: (i, 0, 0, 0)),
        ],
        out_specs=pl.BlockSpec((4, WIDTH, ENT), lambda i: (0, 0, 0)),
        out_shape=jax.ShapeDtypeStruct((4, WIDTH, ENT), F32),
        scratch_shapes=[
            pltpu.VMEM((slots, 512), BF16),
            pltpu.VMEM((slots, 512), BF16),
            pltpu.VMEM((4, ENT, 512), F32),
        ],
        compiler_params=pltpu.CompilerParams(vmem_limit_bytes=VMEM_LIMIT),
        name="row_sum" if octets == MAIN else "row_sum_over",
    )(wanted, arrived)


def entity_kernel(grad_ref, table_ref, state_ref, new_table, new_state):
    grad = (grad_ref[0] + grad_ref[1]) + (grad_ref[2] + grad_ref[3])
    state = state_ref[...] + jnp.sum(grad * grad, axis=0, keepdims=True) / float(WIDTH)
    new_state[...] = state
    new_table[...] = table_ref[...] - learn_rate * grad / (jnp.sqrt(state) + adagrad_eps)


def entity_update(grads, table_t, state):
    return pl.pallas_call(
        entity_kernel,
        out_shape=(
            jax.ShapeDtypeStruct((WIDTH, ENT), F32),
            jax.ShapeDtypeStruct((1, ENT), F32),
        ),
        compiler_params=pltpu.CompilerParams(vmem_limit_bytes=VMEM_LIMIT),
        name="entity_update",
    )(grads, table_t, state)


def relation_update_kernel(
    shard_ref, part_0, part_1, part_2, part_3, table_ref, state_ref, out_ref, table, sem
):
    shard = shard_ref[0]
    group = jnp.minimum(shard >> 1, RELGROUPS - 1)
    lanes = pl.ds(pl.multiple_of(group * 128, 128), 128)
    copy = pltpu.make_async_copy(table_ref.at[:, lanes], table, sem)
    copy.start()
    odd = (shard & 1) == 1

    packed = (part_0[...] + part_1[...]) + (part_2[...] + part_3[...])
    parts = []
    for t in range(4):
        if t < 3:
            part = packed[t * 8 : t * 8 + 8].reshape(64, 128)
        else:
            rest = packed[24]
            part = jnp.concatenate(
                [rest] + [pltpu.roll(rest, 128 - 16 * q, 1) for q in range(1, 8)], axis=0
            )
        both = jnp.concatenate(
            [jnp.where(odd, 0.0, part), jnp.where(odd, part, 0.0)], axis=0
        ).T
        parts.append(both if t < 3 else both[:16])
    grad = jnp.concatenate(parts, axis=0)
    state = state_ref[pl.ds(group, 1), :]
    state = state + jnp.sum(grad * grad, axis=0, keepdims=True) / float(WIDTH)
    copy.wait()
    new = table[...] - grad * (learn_rate / (jnp.sqrt(state) + adagrad_eps))
    top, bottom = new[: WIDTH // 2], new[WIDTH // 2 :]
    low = lax.broadcasted_iota(I32, (WIDTH // 2, 128), 1) < 64
    even_rows = jnp.where(low, top, pltpu.roll(bottom, 64, 1))
    odd_rows = jnp.where(low, pltpu.roll(top, 64, 1), bottom)
    out_ref[0:25] = jnp.where(odd, odd_rows, even_rows).reshape(25, 8, 128)
    out_ref[25] = jnp.broadcast_to(state, (8, 128))


def relation_update(shard, parts, table_t, state):
    return pl.pallas_call(
        relation_update_kernel,
        in_specs=[
            pl.BlockSpec(memory_space=pltpu.SMEM),
            *[pl.BlockSpec(memory_space=pltpu.VMEM)] * 4,
            pl.BlockSpec(memory_space=pl.ANY),
            pl.BlockSpec(memory_space=pltpu.VMEM),
        ],
        out_specs=pl.BlockSpec(memory_space=pltpu.VMEM),
        out_shape=jax.ShapeDtypeStruct((26, 8, 128), F32),
        scratch_shapes=[pltpu.VMEM((WIDTH, 128), F32), pltpu.SemaphoreType.DMA],
        compiler_params=pltpu.CompilerParams(vmem_limit_bytes=VMEM_LIMIT),
        name="relation_update",
    )(shard, *parts, table_t, state)


def unpack_kernel(shards_ref, new_table, new_state):
    low = lax.broadcasted_iota(I32, (WIDTH // 2, 128), 1) < 64
    for g in range(4):
        lanes = slice(g * 128, (g + 1) * 128)
        even = shards_ref[2 * g, 0, 0, 0:25].reshape(WIDTH // 2, 128)
        odd = shards_ref[2 * g + 1, 0, 0, 0:25].reshape(WIDTH // 2, 128)
        new_table[: WIDTH // 2, lanes] = jnp.where(low, even, pltpu.roll(odd, 64, 1))
        new_table[WIDTH // 2 :, lanes] = jnp.where(low, pltpu.roll(even, 64, 1), odd)
        state = jnp.where(low[:8], shards_ref[2 * g, 0, 0, 25], shards_ref[2 * g + 1, 0, 0, 25])
        group = pl.program_id(0) * 4 + g

        @pl.when(group < RELGROUPS)
        def _():
            new_state[pl.ds(group, 1), :] = state[0:1]


def unpack(shards):
    return pl.pallas_call(
        unpack_kernel,
        grid=(pl.cdiv(RELGROUPS, 4),),
        in_specs=[
            pl.BlockSpec(
                (8, 1, 1, 26, 8, 128), lambda i: (i & 1, i >> 3, (i >> 1) & 3, 0, 0, 0)
            )
        ],
        out_specs=(
            pl.BlockSpec((WIDTH, 512), lambda i: (0, i)),
            pl.BlockSpec((RELGROUPS, 128), lambda i: (0, 0)),
        ),
        out_shape=(
            jax.ShapeDtypeStruct((WIDTH, REL), F32),
            jax.ShapeDtypeStruct((RELGROUPS, 128), F32),
        ),
        compiler_params=pltpu.CompilerParams(vmem_limit_bytes=VMEM_LIMIT),
        name="unpack",
    )(shards)


def exchange(x, axis):
    return lax.all_to_all(x, axis, split_axis=0, concat_axis=0, tiled=True)


def any_device(flag):
    largest = flag
    for k in (1, 2, 3):
        moved = lax.ppermute(flag, "rep", [(p, (p + k) % 4) for p in range(4)])
        largest = jnp.maximum(largest, moved)
    return largest


def per_device(
    entity_table,
    entity_state,
    relation_table,
    relation_state,
    end_owner,
    end_row,
    relation_id,
    negative_owner,
    negative_row,
):
    table_t = entity_table.T
    to_right = [(p, (p + 1) % 4) for p in range(4)]
    to_left = [(p, (p + 3) % 4) for p in range(4)]
    left = lax.ppermute(table_t, "rep", to_right)
    right = lax.ppermute(table_t, "rep", to_left)
    rows_at, rep_at = lax.axis_index("rows"), lax.axis_index("rep")
    request, addr = prep(
        rep_at.reshape(1),
        end_owner.T, end_row.T, negative_owner.reshape(1, NEG), negative_row.reshape(8, 128)
    )
    wanted = exchange(request.reshape(GROUP, 2, 128), "rows")
    left, right, _ = lax.optimization_barrier((left, right, wanted))
    across_a = lax.ppermute(left[: WIDTH // 2], "rep", to_right)
    across_b = lax.ppermute(right[WIDTH // 2 :], "rep", to_left)
    tables = (table_t, right, across_a, across_b, left)
    wanted_rows = wanted.reshape(2 * GROUP, 128)
    looked = lookup(MAIN, 0, wanted_rows, tables)
    arrived = exchange(looked, "rows")
    flag = any_device(jnp.max(wanted[:, 1, FLAG]).reshape(1))
    over_now = flag[0] > 0
    core = rows_at & 1
    swap = [(r, r ^ 1) for r in range(GROUP)]
    other_id = lax.ppermute(relation_id, "rows", swap)

    def places(ids):
        near = ids - core * (SHARDS * 64)
        near = jnp.where((near >= 0) & (near < SHARDS * 64), near, SHARDS * 64)
        return ((near >> 3) * 32 + (near & 7)).reshape(8, 128)

    rel_rows = jnp.pad(relation_table[relation_id], ((0, 0), (0, 112)))
    my_places, other_places = places(relation_id), places(other_id)
    rel_rows, my_places, other_places = lax.optimization_barrier(
        (rel_rows, my_places, other_places)
    )
    grads, rel_grads = lax.cond(
        over_now,
        lambda x: math(
            addr, flag, x, exchange(lookup(OVER, MAIN, wanted_rows, tables), "rows"), rel_rows
        ),
        lambda x: math(addr, flag, x, x, rel_rows),
        arrived,
    )
    other_grads = lax.ppermute(rel_grads, "rows", swap)
    outgoing, outgoing_over = pack_grads(addr, flag, grads)
    incoming = exchange(outgoing, "rows")
    rel_grads, other_grads, _ = lax.optimization_barrier((rel_grads, other_grads, outgoing))
    relation_grad = relation_sum(my_places, other_places, rel_grads, other_grads)
    part_grad = lax.psum_scatter(
        relation_grad.reshape(4, 16, 25, 8, 128), "rep", scatter_dimension=0, tiled=True
    )
    part = part_grad.reshape(4, 4, 25, 8, 128)
    y_at, z_at = rows_at >> 3, (rows_at >> 1) & 3
    pieces = [
        lax.dynamic_index_in_dim(part, (y_at + k) & 3, 0, keepdims=False) for k in range(4)
    ]
    part = pieces[0]
    for k in range(1, 4):
        ring = [(r, (r + 8 * k) % GROUP) for r in range(GROUP)]
        part = part + lax.ppermute(pieces[k], "rows", ring)
    pieces = [
        lax.dynamic_index_in_dim(part, (z_at + k) & 3, 0, keepdims=False) for k in range(4)
    ]
    parts = [pieces[0]]
    for k in range(1, 4):
        ring = [(r, r // 8 * 8 + (r + 2 * k) % 8) for r in range(GROUP)]
        parts.append(lax.ppermute(pieces[k], "rows", ring))
    new_shard = relation_update(
        (core * SHARDS + rep_at * 16 + (rows_at >> 1)).reshape(1),
        parts,
        relation_table.T,
        relation_state.reshape(RELGROUPS, 128),
    )
    shards = lax.all_gather(new_shard, AXES, axis=0, tiled=False)
    slots = wanted.reshape(GROUP, 256)

    def ids(first, octets):
        part = slots[:, first * 8 : (first + octets) * 8]
        return part.reshape(GROUP // SUM_STEP, 1, SUM_STEP * octets * 8)

    summed = row_sum(MAIN, ids(0, MAIN), incoming)
    summed = lax.cond(
        over_now,
        lambda x: x + row_sum(OVER, ids(MAIN, OVER), exchange(outgoing_over, "rows")),
        lambda x: x,
        summed,
    )
    entity_grads = exchange(jnp.roll(summed, rep_at, axis=0), "rep")
    new_entity_table, new_entity_state = entity_update(
        entity_grads, table_t, entity_state.reshape(1, ENT)
    )
    new_relation_table, new_relation_state = unpack(shards.reshape(16, 2, 4, 26, 8, 128))
    return (
        new_entity_table.T,
        new_entity_state.reshape(ENT),
        new_relation_table.T,
        new_relation_state.reshape(REL),
    )


def solution(mesh):
    return jax.shard_map(
        per_device,
        mesh=mesh,
        in_specs=(
            P(AXES, None),
            P(AXES),
            P(),
            P(),
            P(AXES, None),
            P(AXES, None),
            P(AXES),
            P(AXES, None),
            P(AXES),
        ),
        out_specs=(P(AXES, None), P(AXES), P(), P()),
        check_vma=False,
    )
```

```python
import functools
import jax
import jax.numpy as jnp
from jax import lax
from jax.experimental import pallas as pl
from jax.experimental.pallas import tpu as pltpu
from jax.sharding import PartitionSpec as P


learn_rate = 0.5
adagrad_eps = 1e-10

AXES = ("rows", "rep")
F32, BF16, I32 = jnp.float32, jnp.bfloat16, jnp.int32
ENT = 512
WIDTH = 400
EDGE = 1024
NEG = 1024
GROUP = 32
MAIN = 23
OCT = 28
OVER = OCT - MAIN
MAIN_TILES = 3 * MAIN + 3
OVER_TILES = 3 * OVER + 1
REL = 7424
RELGROUPS = REL // 128
SHARDS = 64
VMEM_LIMIT = 60 * 1024 * 1024
FLAG = 127
COUNT = 126


def dot(a, b, dims):
    return lax.dot_general(a, b, (dims, ((), ())), preferred_element_type=F32)


NN = ((1,), (0,))
NT = ((1,), (1,))
TN = ((0,), (0,))


def split(x):
    hi = x.astype(BF16)
    return hi, (x - hi.astype(F32)).astype(BF16)


def prep_kernel(me_ref, end_owner, end_row, neg_owner, neg_row, request_ref, addr_ref):
    iota0 = lax.broadcasted_iota(I32, (128, 128), 0)
    upper = (iota0 < lax.broadcasted_iota(I32, (128, 128), 1)).astype(BF16)
    group = lax.broadcasted_iota(I32, (GROUP, 128), 0)
    double = lax.broadcasted_iota(I32, (2 * GROUP, 128), 0)
    count = jnp.zeros((GROUP, 1), F32)
    low = jnp.zeros((2 * GROUP, 128), F32)
    high = jnp.zeros((2 * GROUP, 128), F32)
    for i in range(24):
        lanes = slice((i & 7) * 128, (i & 7) * 128 + 128)
        if i < 16:
            owner = end_owner[i >> 3 : (i >> 3) + 1, lanes]
            row = end_row[i >> 3 : (i >> 3) + 1, lanes]
        else:
            owner = neg_owner[:, lanes]
            row = neg_row[i - 16 : i - 15, :]
        target = owner >> 2
        near = (owner - me_ref[0]) & 3
        value = near * (4 * ENT) + (row >> 3) * 32 + (row & 7)
        onehot = (group == target).astype(F32)
        earlier = dot(onehot.astype(BF16), upper, NN) + count
        rank = jnp.sum(onehot * earlier, axis=0, keepdims=True).astype(I32)
        count = count + jnp.sum(onehot, axis=1, keepdims=True)
        wide = (double == 2 * target + (rank >> 7)).astype(F32).astype(BF16)
        at = iota0 == (rank & 127)
        low = low + dot(wide, jnp.where(at, (value & 255).astype(F32), 0.0).astype(BF16), NT)
        high = high + dot(wide, jnp.where(at, (value >> 8).astype(F32), 0.0).astype(BF16), NT)
        addr_ref[i : i + 1, :] = (target * OCT + (rank >> 3)) * 32 + (rank & 7)
    most = jnp.max(count, axis=0, keepdims=True)
    flag = (most > 8.0 * MAIN).astype(F32)
    lane = lax.broadcasted_iota(I32, (2 * GROUP, 128), 1)
    mark = (lane == FLAG) & ((double & 1) == 1)
    pair = lax.broadcasted_iota(I32, (2 * GROUP, GROUP), 0) >> 1
    same = pair == lax.broadcasted_iota(I32, (2 * GROUP, GROUP), 1)
    half = (2.0 * jnp.floor(count * 0.5), count)
    low_count = half[1] - half[0]
    counts = dot(same.astype(F32).astype(BF16), (half[0] * 0.5).astype(BF16), NN) * 2.0
    counts = counts + dot(same.astype(F32).astype(BF16), low_count.astype(BF16), NN)
    request = jnp.where(mark, flag, low + 256.0 * high)
    mark = (lane == COUNT) & ((double & 1) == 1)
    request_ref[...] = jnp.where(mark, counts, request).astype(I32)


def prep(me, end_owner, end_row, neg_owner, neg_row):
    return pl.pallas_call(
        prep_kernel,
        out_shape=(
            jax.ShapeDtypeStruct((2 * GROUP, 128), I32),
            jax.ShapeDtypeStruct((24, 128), I32),
        ),
        in_specs=[pl.BlockSpec(memory_space=pltpu.SMEM)]
        + [pl.BlockSpec(memory_space=pltpu.VMEM)] * 4,
        name="prep",
    )(me, end_owner, end_row, neg_owner, neg_row)


STEP = 4


def lookup_kernel(
    octets, first, wanted_ref, own, right, across_a, across_b, left, out_ref, table, rows
):
    step = pl.program_id(0)

    @pl.when(step == 0)
    def _():
        def turn(b, _):
            lanes = pl.ds(pl.multiple_of(b * 128, 128), 128)
            for i, parts in enumerate(((own,), (right,), (across_a, across_b), (left,))):
                height = WIDTH // len(parts)
                for t in range(4):
                    pieces, low, high = [], t * 128, min(t * 128 + 128, WIDTH)
                    for n, part in enumerate(parts):
                        start, stop = max(low, n * height), min(high, (n + 1) * height)
                        if start < stop:
                            pieces.append(part[start - n * height : stop - n * height, lanes])
                    if t == 3:
                        pieces.append(jnp.zeros((112, 128), F32))
                    block = pieces[0] if len(pieces) == 1 else jnp.concatenate(pieces, axis=0)
                    table[pl.ds(i * 64 + b * 16, 16), t] = block.T.reshape(16, 8, 128)
            return 0

        lax.fori_loop(0, 4, turn, 0)

    flat = table.reshape(256 * 32, 128)
    rows_flat = rows.reshape(STEP * octets * 32, 128)
    for d in range(STEP):
        g = step * STEP + d
        used = (wanted_ref[2 * g + 1, COUNT] + 7) >> 3
        used = jnp.clip(used - first, 0, octets)

        def fetch(q, _):
            k = (q + first) * 8
            line, lane = 2 * g + (k >> 7), k & 127
            for j in range(8):
                a = wanted_ref[line, lane + j]
                rows_flat[pl.ds((d * octets + q) * 32 + j, 4, stride=8), :] = flat[
                    pl.ds(a, 4, stride=8), :
                ]
            return 0

        lax.fori_loop(0, used, fetch, 0)

        def blank(q, _):
            rows[d, q, 3] = jnp.zeros((8, 128), F32)
            return 0

        lax.fori_loop(used, octets, blank, 0)
    for q in range(octets):
        out_ref[:, 3 * q : 3 * q + 3] = rows[:, q, 0:3]
    for tile in range((octets + 7) // 8):
        rest = rows[:, tile * 8, 3]
        for q in range(tile * 8 + 1, min(octets, tile * 8 + 8)):
            rest = rest + pltpu.roll(rows[:, q, 3], 16 * (q & 7), 2)
        out_ref[:, 3 * octets + tile] = rest


def lookup(octets, first, wanted, tables):
    tiles = 3 * octets + (octets + 7) // 8
    return pl.pallas_call(
        functools.partial(lookup_kernel, octets, first),
        grid=(GROUP // STEP,),
        in_specs=[pl.BlockSpec(memory_space=pltpu.SMEM)]
        + [pl.BlockSpec(x.shape, lambda i: (0, 0)) for x in tables],
        out_specs=pl.BlockSpec((STEP, tiles, 8, 128), lambda i: (i, 0, 0, 0)),
        out_shape=jax.ShapeDtypeStruct((GROUP, tiles, 8, 128), F32),
        scratch_shapes=[
            pltpu.VMEM((256, 4, 8, 128), F32),
            pltpu.VMEM((STEP, octets, 4, 8, 128), F32),
        ],
        compiler_params=pltpu.CompilerParams(vmem_limit_bytes=VMEM_LIMIT),
        name="lookup" if first == 0 else "lookup_over",
    )(wanted, *tables)


BLOCK = 256


def math_kernel(
    addr_ref, flag_ref, pay_ref, over_ref, rel_ref, grad_ref, rel_grad_ref,
    rows, rest, hr_hi, hr_lo, n_hi, n_lo, g_neg, sems,
):
    def fill(source, octets, first, tile, sem):
        copies = [
            pltpu.make_async_copy(
                source.at[:, 3 * q : 3 * q + 3], rows.at[:, first + q, 0:3], sems.at[sem + 1 + q]
            )
            for q in range(octets)
        ]
        tiles = (octets + 7) // 8
        last = pltpu.make_async_copy(
            source.at[:, 3 * octets : 3 * octets + tiles],
            rest.at[:, tile : tile + tiles],
            sems.at[sem],
        )
        last.start()
        for copy in copies:
            copy.start()
        last.wait()
        lane = lax.broadcasted_iota(I32, (8, 8, 128), 2)

        def expand(i, _):
            for q in range(octets):
                part = rest[pl.ds(i * 8, 8), tile + (q >> 3)]
                if q & 7:
                    part = pltpu.roll(part, 128 - 16 * (q & 7), 2)
                rows[pl.ds(i * 8, 8), first + q, 3] = jnp.where(lane < 16, part, 0.0)
            return 0

        lax.fori_loop(0, GROUP // 8, expand, 0)
        for copy in copies:
            copy.wait()

    fill(pay_ref, MAIN, 0, 0, 0)

    @pl.when(flag_ref[0] > 0)
    def _():
        fill(over_ref, OVER, MAIN, 3, MAIN + 1)

    flat = rows.reshape(GROUP * OCT * 32, 128)
    grad_flat = grad_ref.reshape(384 * 32, 128)

    def gather(i, _):
        for j in range(8):
            a = addr_ref[i >> 4, (i & 15) * 8 + j]
            grad_flat[pl.ds(i * 32 + j, 4, stride=8), :] = flat[pl.ds(a, 4, stride=8), :]
        return 0

    lax.fori_loop(0, 384, gather, 0, unroll=4)

    def prepare(b, _):
        octets = pl.ds(b * 32, 32)
        edges = pl.ds(b * BLOCK, BLOCK)
        for t in range(4):
            lanes = slice(t * 128, (t + 1) * 128)
            hr = grad_ref[octets, t].reshape(BLOCK, 128) * rel_ref[edges, lanes]
            hr_hi[edges, lanes], hr_lo[edges, lanes] = split(hr)
            neg = grad_ref[pl.ds(256 + b * 32, 32), t].reshape(BLOCK, 128)
            n_hi[edges, lanes], n_lo[edges, lanes] = split(neg)
        return 0

    lax.fori_loop(0, EDGE // BLOCK, prepare, 0)
    g_neg[...] = jnp.zeros_like(g_neg)

    def block(b, _):
        edges = pl.ds(b * BLOCK, BLOCK)
        octets = pl.ds(b * 32, 32)
        tails = pl.ds(128 + b * 32, 32)
        a_hi, a_lo = hr_hi[edges, :], hr_lo[edges, :]
        score = dot(a_hi, n_hi[...], NT) + dot(a_hi, n_lo[...], NT) + dot(a_lo, n_hi[...], NT)
        p_hi, p_lo = split(1.0 / (1.0 + jnp.exp(-score)))
        g_hr = dot(p_hi, n_hi[...], NN) + dot(p_hi, n_lo[...], NN) + dot(p_lo, n_hi[...], NN)
        g_neg[...] += dot(p_hi, a_hi, TN) + dot(p_hi, a_lo, TN) + dot(p_lo, a_hi, TN)
        total = jnp.zeros((BLOCK, 128), F32)
        for t in range(4):
            lanes = slice(t * 128, (t + 1) * 128)
            hr = grad_ref[octets, t].reshape(BLOCK, 128) * rel_ref[edges, lanes]
            total = total + hr * grad_ref[tails, t].reshape(BLOCK, 128)
        positive = jnp.sum(total, axis=1, keepdims=True)
        d_pos = -1.0 / (1.0 + jnp.exp(positive))
        for t in range(4):
            lanes = slice(t * 128, (t + 1) * 128)
            head = grad_ref[octets, t].reshape(BLOCK, 128)
            tail = grad_ref[tails, t].reshape(BLOCK, 128)
            rel = rel_ref[edges, lanes]
            g = d_pos * tail + g_hr[:, lanes] * (1.0 / NEG)
            rel_grad_ref[octets, t] = (g * head).reshape(32, 8, 128)
            grad_ref[tails, t] = (d_pos * (head * rel)).reshape(32, 8, 128)
            grad_ref[octets, t] = (g * rel).reshape(32, 8, 128)
        return 0

    lax.fori_loop(0, EDGE // BLOCK, block, 0)
    for t in range(4):
        lanes = slice(t * 128, (t + 1) * 128)
        grad_ref[256:384, t] = (g_neg[:, lanes] * (1.0 / NEG)).reshape(128, 8, 128)


def math(addr, flag, arrived, over, rel_rows):
    return pl.pallas_call(
        math_kernel,
        in_specs=[
            pl.BlockSpec(memory_space=pltpu.SMEM),
            pl.BlockSpec(memory_space=pltpu.SMEM),
            pl.BlockSpec(memory_space=pl.ANY),
            pl.BlockSpec(memory_space=pl.ANY),
            pl.BlockSpec(memory_space=pltpu.VMEM),
        ],
        out_specs=(
            pl.BlockSpec(memory_space=pltpu.VMEM),
            pl.BlockSpec(memory_space=pltpu.VMEM),
        ),
        out_shape=(
            jax.ShapeDtypeStruct((384, 4, 8, 128), F32),
            jax.ShapeDtypeStruct((128, 4, 8, 128), F32),
        ),
        scratch_shapes=[
            pltpu.VMEM((GROUP, OCT, 4, 8, 128), F32),
            pltpu.VMEM((GROUP, 4, 8, 128), F32),
            pltpu.VMEM((EDGE, 512), BF16),
            pltpu.VMEM((EDGE, 512), BF16),
            pltpu.VMEM((NEG, 512), BF16),
            pltpu.VMEM((NEG, 512), BF16),
            pltpu.VMEM((NEG, 512), F32),
            pltpu.SemaphoreType.DMA((OCT + 2,)),
        ],
        compiler_params=pltpu.CompilerParams(vmem_limit_bytes=VMEM_LIMIT),
        name="math",
    )(addr, flag, arrived, over, rel_rows)


def relation_kernel(id_ref, other_id_ref, grad_ref, other_ref, out_ref, mine, others, packed, sems):
    zero = jnp.zeros((8, 4, 8, 128), F32)

    def clear(g, _):
        mine[pl.ds(g * 8, 8)] = zero
        others[pl.ds(g * 8, 8)] = zero
        return 0

    lax.fori_loop(0, SHARDS + 1, clear, 0)
    height = (SHARDS + 1) * 256
    sides = (
        (id_ref, grad_ref.reshape(128 * 32, 128), mine.reshape(height, 128)),
        (other_id_ref, other_ref.reshape(128 * 32, 128), others.reshape(height, 128)),
    )

    def add(i, _):
        for j in range(8):
            for ids, grad, flat in sides:
                at = pl.ds(ids[i >> 4, (i & 15) * 8 + j], 4, stride=8)
                flat[at, :] = flat[at, :] + grad[pl.ds(i * 32 + j, 4, stride=8), :]
        return 0

    lax.fori_loop(0, 128, add, 0)

    def copy(g):
        return pltpu.make_async_copy(
            packed.at[g & 1], out_ref.at[pl.ds(g * 4, 4)], sems.at[g & 1]
        )

    def pack(g, _):
        @pl.when(g >= 2)
        def _():
            copy(g - 2).wait()

        for n in range(4):
            first = g * 32 + n * 8
            for t in range(3):
                packed[g & 1, n, t * 8 : t * 8 + 8] = (
                    mine[pl.ds(first, 8), t] + others[pl.ds(first, 8), t]
                )
            rest = mine[first, 3] + others[first, 3]
            for q in range(1, 8):
                rest = rest + pltpu.roll(mine[first + q, 3] + others[first + q, 3], 16 * q, 1)
            packed[g & 1, n, 24] = rest
        copy(g).start()
        return 0

    lax.fori_loop(0, SHARDS // 4, pack, 0)
    copy(SHARDS // 4 - 2).wait()
    copy(SHARDS // 4 - 1).wait()


def relation_sum(ids, other_ids, grad, other):
    return pl.pallas_call(
        relation_kernel,
        in_specs=[
            pl.BlockSpec(memory_space=pltpu.SMEM),
            pl.BlockSpec(memory_space=pltpu.SMEM),
            pl.BlockSpec(memory_space=pltpu.VMEM),
            pl.BlockSpec(memory_space=pltpu.VMEM),
        ],
        out_specs=pl.BlockSpec(memory_space=pl.ANY),
        out_shape=jax.ShapeDtypeStruct((SHARDS, 25, 8, 128), F32),
        scratch_shapes=[
            pltpu.VMEM(((SHARDS + 1) * 8, 4, 8, 128), F32),
            pltpu.VMEM(((SHARDS + 1) * 8, 4, 8, 128), F32),
            pltpu.VMEM((2, 4, 25, 8, 128), F32),
            pltpu.SemaphoreType.DMA((2,)),
        ],
        compiler_params=pltpu.CompilerParams(vmem_limit_bytes=VMEM_LIMIT),
        name="relation_sum",
    )(ids, other_ids, grad, other)


def pack_kernel(addr_ref, flag_ref, grad_ref, out_ref, over_ref, rows, rest, sems):
    zero = jnp.zeros((2, OCT, 4, 8, 128), F32)

    def clear(i, _):
        rows[pl.ds(i * 2, 2)] = zero
        return 0

    lax.fori_loop(0, GROUP // 2, clear, 0)
    flat = rows.reshape(GROUP * OCT * 32, 128)
    grad_flat = grad_ref.reshape(384 * 32, 128)

    def scatter(i, _):
        for j in range(8):
            a = addr_ref[i >> 4, (i & 15) * 8 + j]
            flat[pl.ds(a, 4, stride=8), :] = grad_flat[pl.ds(i * 32 + j, 4, stride=8), :]
        return 0

    lax.fori_loop(0, 384, scatter, 0, unroll=4)

    def send(target, octets, first, tile, sem):
        copies = [
            pltpu.make_async_copy(
                rows.at[:, first + q, 0:3], target.at[:, 3 * q : 3 * q + 3], sems.at[sem + 1 + q]
            )
            for q in range(octets)
        ]
        for copy in copies:
            copy.start()
        tiles = (octets + 7) // 8

        def pack(i, _):
            at = pl.ds(i * 8, 8)
            for n in range(tiles):
                part = rows[at, first + n * 8, 3]
                for q in range(n * 8 + 1, min(octets, n * 8 + 8)):
                    part = part + pltpu.roll(rows[at, first + q, 3], 16 * (q & 7), 2)
                rest[at, tile + n] = part
            return 0

        lax.fori_loop(0, GROUP // 8, pack, 0)
        last = pltpu.make_async_copy(
            rest.at[:, tile : tile + tiles],
            target.at[:, 3 * octets : 3 * octets + tiles],
            sems.at[sem],
        )
        last.start()
        for copy in copies:
            copy.wait()
        last.wait()

    send(out_ref, MAIN, 0, 0, 0)

    @pl.when(flag_ref[0] > 0)
    def _():
        send(over_ref, OVER, MAIN, 3, MAIN + 1)


def pack_grads(addr, flag, grads):
    return pl.pallas_call(
        pack_kernel,
        in_specs=[
            pl.BlockSpec(memory_space=pltpu.SMEM),
            pl.BlockSpec(memory_space=pltpu.SMEM),
            pl.BlockSpec(memory_space=pltpu.VMEM),
        ],
        out_specs=(
            pl.BlockSpec(memory_space=pl.ANY),
            pl.BlockSpec(memory_space=pl.ANY),
        ),
        out_shape=(
            jax.ShapeDtypeStruct((GROUP, MAIN_TILES, 8, 128), F32),
            jax.ShapeDtypeStruct((GROUP, OVER_TILES, 8, 128), F32),
        ),
        scratch_shapes=[
            pltpu.VMEM((GROUP, OCT, 4, 8, 128), F32),
            pltpu.VMEM((GROUP, 4, 8, 128), F32),
            pltpu.SemaphoreType.DMA((OCT + 2,)),
        ],
        compiler_params=pltpu.CompilerParams(vmem_limit_bytes=VMEM_LIMIT),
        name="pack_grads",
    )(addr, flag, grads)


SUM_STEP = 8


def row_sum_kernel(octets, wanted_ref, pay_ref, out_ref, hi, lo, total):
    step = pl.program_id(0)
    slots = SUM_STEP * octets * 8

    @pl.when(step == 0)
    def _():
        total[...] = jnp.zeros_like(total)

    lane = lax.broadcasted_iota(I32, (SUM_STEP, 8, 128), 2)
    for t in range(4):
        lanes = slice(t * 128, (t + 1) * 128)
        parts = []
        for q in range(octets):
            if t < 3:
                parts.append(pay_ref[:, q * 3 + t])
            else:
                part = pay_ref[:, 3 * octets + (q >> 3)]
                if q & 7:
                    part = pltpu.roll(part, 128 - 16 * (q & 7), 2)
                parts.append(jnp.where(lane < 16, part, 0.0))
        hi[:, lanes], lo[:, lanes] = split(jnp.stack(parts, axis=1).reshape(slots, 128))
    wanted = wanted_ref[...].reshape(1, slots)

    def add(i, _):
        row = lax.broadcasted_iota(I32, (ENT, slots), 0)
        row = i * (4 * ENT) + (row >> 3) * 32 + (row & 7)
        onehot = (row == wanted).astype(F32).astype(BF16)
        total[i] = total[i] + (dot(onehot, hi[...], NN) + dot(onehot, lo[...], NN))
        return 0

    lax.fori_loop(0, 4, add, 0)

    @pl.when(step == pl.num_programs(0) - 1)
    def _():
        def turn(i, _):
            out_ref[i] = total[i].T[:WIDTH, :]
            return 0

        lax.fori_loop(0, 4, turn, 0)


def row_sum(octets, wanted, arrived):
    tiles = 3 * octets + (octets + 7) // 8
    slots = SUM_STEP * octets * 8
    return pl.pallas_call(
        functools.partial(row_sum_kernel, octets),
        grid=(GROUP // SUM_STEP,),
        in_specs=[
            pl.BlockSpec((1, 1, slots), lambda i: (i, 0, 0)),
            pl.BlockSpec((SUM_STEP, tiles, 8, 128), lambda i: (i, 0, 0, 0)),
        ],
        out_specs=pl.BlockSpec((4, WIDTH, ENT), lambda i: (0, 0, 0)),
        out_shape=jax.ShapeDtypeStruct((4, WIDTH, ENT), F32),
        scratch_shapes=[
            pltpu.VMEM((slots, 512), BF16),
            pltpu.VMEM((slots, 512), BF16),
            pltpu.VMEM((4, ENT, 512), F32),
        ],
        compiler_params=pltpu.CompilerParams(vmem_limit_bytes=VMEM_LIMIT),
        name="row_sum" if octets == MAIN else "row_sum_over",
    )(wanted, arrived)


def entity_kernel(grad_ref, table_ref, state_ref, new_table, new_state):
    grad = (grad_ref[0] + grad_ref[1]) + (grad_ref[2] + grad_ref[3])
    state = state_ref[...] + jnp.sum(grad * grad, axis=0, keepdims=True) / float(WIDTH)
    new_state[...] = state
    new_table[...] = table_ref[...] - learn_rate * grad / (jnp.sqrt(state) + adagrad_eps)


def entity_update(grads, table_t, state):
    return pl.pallas_call(
        entity_kernel,
        out_shape=(
            jax.ShapeDtypeStruct((WIDTH, ENT), F32),
            jax.ShapeDtypeStruct((1, ENT), F32),
        ),
        compiler_params=pltpu.CompilerParams(vmem_limit_bytes=VMEM_LIMIT),
        name="entity_update",
    )(grads, table_t, state)


def relation_update_kernel(
    shard_ref, part_0, part_1, part_2, part_3, table_ref, state_ref, out_ref, table, sem
):
    shard = shard_ref[0]
    group = jnp.minimum(shard >> 1, RELGROUPS - 1)
    lanes = pl.ds(pl.multiple_of(group * 128, 128), 128)
    copy = pltpu.make_async_copy(table_ref.at[:, lanes], table, sem)
    copy.start()
    odd = (shard & 1) == 1

    packed = (part_0[...] + part_1[...]) + (part_2[...] + part_3[...])
    parts = []
    for t in range(4):
        if t < 3:
            part = packed[t * 8 : t * 8 + 8].reshape(64, 128)
        else:
            rest = packed[24]
            part = jnp.concatenate(
                [rest] + [pltpu.roll(rest, 128 - 16 * q, 1) for q in range(1, 8)], axis=0
            )
        both = jnp.concatenate(
            [jnp.where(odd, 0.0, part), jnp.where(odd, part, 0.0)], axis=0
        ).T
        parts.append(both if t < 3 else both[:16])
    grad = jnp.concatenate(parts, axis=0)
    state = state_ref[pl.ds(group, 1), :]
    state = state + jnp.sum(grad * grad, axis=0, keepdims=True) / float(WIDTH)
    copy.wait()
    new = table[...] - grad * (learn_rate / (jnp.sqrt(state) + adagrad_eps))
    top, bottom = new[: WIDTH // 2], new[WIDTH // 2 :]
    low = lax.broadcasted_iota(I32, (WIDTH // 2, 128), 1) < 64
    even_rows = jnp.where(low, top, pltpu.roll(bottom, 64, 1))
    odd_rows = jnp.where(low, pltpu.roll(top, 64, 1), bottom)
    out_ref[0:25] = jnp.where(odd, odd_rows, even_rows).reshape(25, 8, 128)
    out_ref[25] = jnp.broadcast_to(state, (8, 128))


def relation_update(shard, parts, table_t, state):
    return pl.pallas_call(
        relation_update_kernel,
        in_specs=[
            pl.BlockSpec(memory_space=pltpu.SMEM),
            *[pl.BlockSpec(memory_space=pltpu.VMEM)] * 4,
            pl.BlockSpec(memory_space=pl.ANY),
            pl.BlockSpec(memory_space=pltpu.VMEM),
        ],
        out_specs=pl.BlockSpec(memory_space=pltpu.VMEM),
        out_shape=jax.ShapeDtypeStruct((26, 8, 128), F32),
        scratch_shapes=[pltpu.VMEM((WIDTH, 128), F32), pltpu.SemaphoreType.DMA],
        compiler_params=pltpu.CompilerParams(vmem_limit_bytes=VMEM_LIMIT),
        name="relation_update",
    )(shard, *parts, table_t, state)


def unpack_kernel(shards_ref, new_table, new_state):
    low = lax.broadcasted_iota(I32, (WIDTH // 2, 128), 1) < 64
    for g in range(4):
        lanes = slice(g * 128, (g + 1) * 128)
        even = shards_ref[2 * g, 0, 0, 0:25].reshape(WIDTH // 2, 128)
        odd = shards_ref[2 * g + 1, 0, 0, 0:25].reshape(WIDTH // 2, 128)
        new_table[: WIDTH // 2, lanes] = jnp.where(low, even, pltpu.roll(odd, 64, 1))
        new_table[WIDTH // 2 :, lanes] = jnp.where(low, pltpu.roll(even, 64, 1), odd)
        state = jnp.where(low[:8], shards_ref[2 * g, 0, 0, 25], shards_ref[2 * g + 1, 0, 0, 25])
        group = pl.program_id(0) * 4 + g

        @pl.when(group < RELGROUPS)
        def _():
            new_state[pl.ds(group, 1), :] = state[0:1]


def unpack(shards):
    return pl.pallas_call(
        unpack_kernel,
        grid=(pl.cdiv(RELGROUPS, 4),),
        in_specs=[
            pl.BlockSpec(
                (8, 1, 1, 26, 8, 128), lambda i: (i & 1, i >> 3, (i >> 1) & 3, 0, 0, 0)
            )
        ],
        out_specs=(
            pl.BlockSpec((WIDTH, 512), lambda i: (0, i)),
            pl.BlockSpec((RELGROUPS, 128), lambda i: (0, 0)),
        ),
        out_shape=(
            jax.ShapeDtypeStruct((WIDTH, REL), F32),
            jax.ShapeDtypeStruct((RELGROUPS, 128), F32),
        ),
        compiler_params=pltpu.CompilerParams(vmem_limit_bytes=VMEM_LIMIT),
        name="unpack",
    )(shards)


def exchange(x, axis):
    return lax.all_to_all(x, axis, split_axis=0, concat_axis=0, tiled=True)


def any_device(flag):
    largest = flag
    for k in (1, 2, 3):
        moved = lax.ppermute(flag, "rep", [(p, (p + k) % 4) for p in range(4)])
        largest = jnp.maximum(largest, moved)
    return largest


def per_device(
    entity_table,
    entity_state,
    relation_table,
    relation_state,
    end_owner,
    end_row,
    relation_id,
    negative_owner,
    negative_row,
):
    table_t = entity_table.T
    to_right = [(p, (p + 1) % 4) for p in range(4)]
    to_left = [(p, (p + 3) % 4) for p in range(4)]
    left = lax.ppermute(table_t, "rep", to_right)
    right = lax.ppermute(table_t, "rep", to_left)
    rows_at, rep_at = lax.axis_index("rows"), lax.axis_index("rep")
    request, addr = prep(
        rep_at.reshape(1),
        end_owner.T, end_row.T, negative_owner.reshape(1, NEG), negative_row.reshape(8, 128)
    )
    wanted = exchange(request.reshape(GROUP, 2, 128), "rows")
    rel_rows = relation_table[relation_id]
    left, right, _, rel_rows = lax.optimization_barrier((left, right, wanted, rel_rows))
    across_a = lax.ppermute(left[: WIDTH // 2], "rep", to_right)
    across_b = lax.ppermute(right[WIDTH // 2 :], "rep", to_left)
    tables = (table_t, right, across_a, across_b, left)
    wanted_rows = wanted.reshape(2 * GROUP, 128)
    looked = lookup(MAIN, 0, wanted_rows, tables)
    flag = any_device(jnp.max(wanted[:, 1, FLAG]).reshape(1))
    core = rows_at & 1
    swap = [(r, r ^ 1) for r in range(GROUP)]
    other_id = lax.ppermute(relation_id, "rows", swap)

    def places(ids):
        near = ids - core * (SHARDS * 64)
        near = jnp.where((near >= 0) & (near < SHARDS * 64), near, SHARDS * 64)
        return ((near >> 3) * 32 + (near & 7)).reshape(8, 128)

    rel_rows = jnp.pad(rel_rows, ((0, 0), (0, 112)))
    my_places, other_places = places(relation_id), places(other_id)
    rel_rows, my_places, other_places = lax.optimization_barrier(
        (rel_rows, my_places, other_places)
    )
    over_now = flag[0] > 0
    looked, rel_rows, flag, over_now = lax.optimization_barrier(
        (looked, rel_rows, flag, over_now)
    )
    arrived = exchange(looked, "rows")
    grads, rel_grads = lax.cond(
        over_now,
        lambda x: math(
            addr, flag, x, exchange(lookup(OVER, MAIN, wanted_rows, tables), "rows"), rel_rows
        ),
        lambda x: math(addr, flag, x, x, rel_rows),
        arrived,
    )
    other_grads = lax.ppermute(rel_grads, "rows", swap)
    outgoing, outgoing_over = pack_grads(addr, flag, grads)
    incoming = exchange(outgoing, "rows")
    rel_grads, other_grads, _ = lax.optimization_barrier((rel_grads, other_grads, outgoing))
    relation_grad = relation_sum(my_places, other_places, rel_grads, other_grads)
    part_grad = lax.psum_scatter(
        relation_grad.reshape(4, 16, 25, 8, 128), "rep", scatter_dimension=0, tiled=True
    )
    part = part_grad.reshape(4, 4, 25, 8, 128)
    y_at, z_at = rows_at >> 3, (rows_at >> 1) & 3
    pieces = [
        lax.dynamic_index_in_dim(part, (y_at + k) & 3, 0, keepdims=False) for k in range(4)
    ]
    parts = [pieces[0]]
    for k in range(1, 4):
        ring = [(r, (r + 8 * k) % GROUP) for r in range(GROUP)]
        parts.append(lax.ppermute(pieces[k], "rows", ring))
    part = (parts[0] + parts[1]) + (parts[2] + parts[3])
    pieces = [
        lax.dynamic_index_in_dim(part, (z_at + k) & 3, 0, keepdims=False) for k in range(4)
    ]
    parts = [pieces[0]]
    for k in range(1, 4):
        ring = [(r, r // 8 * 8 + (r + 2 * k) % 8) for r in range(GROUP)]
        parts.append(lax.ppermute(pieces[k], "rows", ring))
    slots = wanted.reshape(GROUP, 256)

    def ids(first, octets):
        part = slots[:, first * 8 : (first + octets) * 8]
        return part.reshape(GROUP // SUM_STEP, 1, SUM_STEP * octets * 8)

    summed = row_sum(MAIN, ids(0, MAIN), incoming)
    summed, parts = lax.optimization_barrier((summed, parts))
    new_shard = relation_update(
        (core * SHARDS + rep_at * 16 + (rows_at >> 1)).reshape(1),
        parts,
        relation_table.T,
        relation_state.reshape(RELGROUPS, 128),
    )
    shards = lax.all_gather(new_shard, AXES, axis=0, tiled=False)
    summed = lax.cond(
        over_now,
        lambda x: x + row_sum(OVER, ids(MAIN, OVER), exchange(outgoing_over, "rows")),
        lambda x: x,
        summed,
    )
    entity_grads = exchange(jnp.roll(summed, rep_at, axis=0), "rep")
    new_entity_table, new_entity_state = entity_update(
        entity_grads, table_t, entity_state.reshape(1, ENT)
    )
    new_relation_table, new_relation_state = unpack(shards.reshape(16, 2, 4, 26, 8, 128))
    return (
        new_entity_table.T,
        new_entity_state.reshape(ENT),
        new_relation_table.T,
        new_relation_state.reshape(REL),
    )


def solution(mesh):
    return jax.shard_map(
        per_device,
        mesh=mesh,
        in_specs=(
            P(AXES, None),
            P(AXES),
            P(),
            P(),
            P(AXES, None),
            P(AXES, None),
            P(AXES),
            P(AXES, None),
            P(AXES),
        ),
        out_specs=(P(AXES, None), P(AXES), P(), P()),
        check_vma=False,
    )
```
